128 devices in a mesh: row: 8 (over z, x_hi), col: 16 (over y, x_lo, core).
Axes of the slice: x: 4 (x_hi: 2, x_lo: 2; x = x_hi * 2 + x_lo), y: 4, z: 4, core: 2. Of those that a mesh axis runs over, the one named last changes fastest.
Arguments:
- features: bfloat16 [32768, 512], P('row'), may hold values from -6 to 6
- logits: float32 [32768, 128], P(('row', 'col')), may hold values from -16 to 16
Outputs:
- memberships: float32 [32768, 128], P(('row', 'col'))
- standardized: float32 [32768, 128], P(('row', 'col'))
The draws below stay inside these ranges and needn't reach their ends.
All inputs are finite; a program needn't handle non-finite values.
Results may differ from the reference program's by a relative error of at most 0.0003.
Values may be sent and summed in bfloat16 or wider, within the bound.
A program may use at most 64 MiB of HBM per device.

```python
import math
import jax
import jax.numpy as jnp
from jax import lax

F = 512
C = 128
ITERS = 2
N = 32768


def block_levels(rng, extent, split, smallest, top_value):
    loudness = 1.0
    for dim, shards_of in split:
        heights = jax.random.uniform(jax.random.fold_in(jax.random.fold_in(rng, 6), dim), (shards_of,), jnp.float32, smallest / len(split), top_value / len(split))
        loudness = loudness * jnp.repeat(jnp.exp(heights), extent[dim] // shards_of).reshape((-1,) + (1,) * (len(extent) - 1 - dim))
    return loudness


def gaussian(key, dims, scale, limit, shards=(), held_as=jnp.bfloat16):
    drawn = scale * jax.random.normal(key, dims, jnp.float32)
    if shards:
        drawn = drawn * block_levels(key, dims, shards, -0.22, 0.18)
    return jnp.clip(drawn, -limit, limit).astype(held_as)


def setup_inputs(seed: int = 0) -> dict:
    seeds = jax.random.split(jax.random.key(seed), 3)
    features = gaussian(seeds[0], (N, F), 1.0, 6.0, ((0, 8),))
    logits = gaussian(seeds[1], (N, C), 3.0, 16.0, ((0, 128),), jnp.float32)
    return {"features": features, "logits": logits}


def kernel_scores(features, members):
    total = features.shape[0]
    feature_width = features.shape[1]
    block_rows = math.gcd(total, 512)
    blocks = features.reshape(total // block_rows, block_rows, feature_width)

    def block_product(block):
        inner = jnp.dot(block, features.T, preferred_element_type=jnp.float32)
        base = 1.0 + inner / feature_width
        kernel = base * base * base
        return jnp.dot(kernel, members, precision=lax.Precision.HIGHEST, preferred_element_type=jnp.float32)
    return lax.map(block_product, blocks).reshape(total, members.shape[1])

def reference(features, logits):
    raised = jnp.exp(logits)
    members = raised / lax.optimization_barrier(jnp.sum(raised, axis=1, keepdims=True))
    standardized = members
    for iteration in range(ITERS):
        scores = kernel_scores(features, members)
        cluster_size = lax.optimization_barrier(jnp.sum(members, axis=0))
        weighted = lax.optimization_barrier(jnp.sum(members * scores, axis=0))
        compact = weighted / (cluster_size * cluster_size)
        distance = compact[None, :] - 2.0 * scores / cluster_size[None, :]
        centered = distance - lax.optimization_barrier(jnp.mean(distance, axis=1, keepdims=True))
        spread = lax.optimization_barrier(jnp.mean(centered * centered, axis=1, keepdims=True))
        standardized = centered / jnp.sqrt(spread + 1e-06)
        raised = jnp.exp(-2.0 * standardized)
        members = raised / lax.optimization_barrier(jnp.sum(raised, axis=1, keepdims=True))
    return (members, standardized)
```

```python
import functools

import jax
import jax.numpy as jnp
from jax import lax
from jax.experimental import pallas as pl
from jax.experimental.pallas import tpu as pltpu
from jax.sharding import PartitionSpec as P

ITERS = 2
SUB = 256
MESH = pl.DeviceIdType.MESH
BF16 = jnp.bfloat16
F32 = jnp.float32


def rows(start, size=SUB):
    return pl.ds(start if isinstance(start, int) else pl.multiple_of(start, 128), size)


def softmax_rows(raised):
    return raised / jnp.sum(raised, axis=1, keepdims=True)


def kernel(
    feat, logits, memb_out, std_out,
    frow, fcol, mem0, mem1, p_hi, p_lo, own, total,
    mid, near, side, vec,
    load_sem, f_send, f_recv, m_send, m_recv, r_send, r_recv, v_send, v_recv,
):
    clusters = logits.shape[1]
    width = feat.shape[1]
    row, col = lax.axis_index("row"), lax.axis_index("col")
    z, xh = row // 2, row % 2
    y, xl, core = col // 4, (col // 2) % 2, col % 2

    def device(dz=0, dx1=0, dy=0, dx2=0, dk=0):
        new_xh = (xh + dx1) % 2
        new_xl = (xl + dx1 + dx2) % 2
        return (
            ((z + dz) % 4) * 2 + new_xh,
            ((y + dy) % 4) * 4 + new_xl * 2 + (core + dk) % 2,
        )

    z_up, z_down = device(dz=1), device(dz=3)
    cross, partner = device(dx1=1), device(dk=1)
    y_up, y_down, across = device(dy=1), device(dy=3), device(dx2=1)
    reduce_group = [(dy, dx) for dy in range(4) for dx in range(2)][1:]
    gather_group = [(dz, dx, dk) for dz in range(4) for dx in range(2) for dk in range(2)][1:]

    barrier = pltpu.get_barrier_semaphore()
    for dy, dx in reduce_group:
        pl.semaphore_signal(barrier, inc=1, device_id=device(dy=dy, dx2=dx), device_id_type=MESH)
    for dz, dx, dk in gather_group:
        pl.semaphore_signal(
            barrier, inc=1, device_id=device(dz=dz, dx1=dx, dk=dk), device_id_type=MESH
        )

    order = [(2, 1), (2, 0), (1, 1), (3, 1), (1, 0), (3, 0), (0, 1), (0, 0)]
    loads = []
    for u, (dy, dx) in enumerate(order):
        block = ((y + dy) % 4) * 4 + ((xl + dx) % 2) * 2 + core
        loads.append(
            pltpu.make_async_copy(
                feat.at[rows(block * SUB)], frow.at[rows(u * SUB)], load_sem.at[u]
            )
        )
    loads.append(
        pltpu.make_async_copy(
            feat.at[rows((y * 4 + xl * 2) * SUB, 2 * SUB)], fcol.at[rows(0, 2 * SUB)], load_sem.at[8]
        )
    )
    for load in loads:
        load.start()

    def put_members(members, mem):
        hi = members.astype(BF16)
        lo = (members - hi.astype(F32)).astype(BF16)
        own[...] = members
        mem[rows(core * SUB), 0:clusters] = hi
        mem[rows(core * SUB), clusters : 2 * clusters] = lo

    put_members(softmax_rows(jnp.exp(logits[...])), mem0)
    pl.semaphore_wait(barrier, len(reduce_group) + len(gather_group))

    class Stream:
        def __init__(self, buf, send, recv, own_src=None):
            self.buf, self.send, self.recv = buf, send, recv
            self.own_src = own_src
            self.sent = 0
            self.started = []

        def at(self, slot, half=None, other=False):
            part = 1 - core if other else core
            start = slot * 2 * SUB + part * SUB
            if half is None:
                return self.buf.at[rows(start)]
            return self.buf.at[rows(start + half * (SUB // 2), SUB // 2)]

        def make(self, src, dst, where, sem):
            n = self.sent
            self.sent += 1
            self.started.append((n, src))
            return pltpu.make_async_remote_copy(
                src_ref=src(), dst_ref=dst, send_sem=self.send.at[n], recv_sem=self.recv.at[sem],
                device_id=where, device_id_type=MESH,
            )

        def wait(self, *sems):
            for s in sems:
                if s >= 9:
                    dst = self.at(s - 9, other=True)
                elif s >= 8:
                    dst = self.at(7)
                elif s >= 6:
                    dst = self.at(6, s - 6)
                else:
                    dst = self.at(s)
                pltpu.make_async_copy(dst, dst, self.recv.at[s]).wait()

        def send_own(self):
            src = self.own_src or (lambda: self.at(0))
            self.make(src, self.at(2), z_up, 2).start()
            self.make(src, self.at(3), z_down, 3).start()
            self.make(src, self.at(1), cross, 1).start()
            if self.own_src is None:
                self.make(src, self.at(0), partner, 9).start()

        def to_partner(self, slot):
            self.make(lambda: self.at(slot), self.at(slot), partner, 9 + slot).start()

        def forward_1(self):
            self.wait(1)
            self.make(lambda: self.at(1), self.at(4), z_up, 4).start()
            self.make(lambda: self.at(1), self.at(5), z_down, 5).start()
            self.to_partner(1)

        def forward_2(self):
            self.wait(2)
            self.make(lambda: self.at(2, 0), self.at(6, 0), z_up, 6).start()
            self.to_partner(2)

        def forward_3(self):
            self.wait(3)
            self.make(lambda: self.at(3, 1), self.at(6, 1), z_down, 7).start()
            self.to_partner(3)

        def forward_45(self):
            self.wait(4)
            self.to_partner(4)
            self.wait(5)
            self.to_partner(5)

        def forward_6(self):
            self.wait(6, 7)
            self.make(lambda: self.at(6), self.at(7), cross, 8).start()
            self.to_partner(6)

        def forward_7(self):
            self.wait(8)
            self.to_partner(7)

        def finish(self):
            for n, src in self.started:
                pltpu.make_async_copy(src(), src(), self.send.at[n]).wait()

    feats = Stream(fcol, f_send, f_recv, lambda: feat.at[rows(col * SUB)])
    mems = [
        Stream(mem, m_send.at[i], m_recv.at[i]) for i, mem in enumerate((mem0, mem1))
    ]
    feats.send_own()
    mems[0].send_own()

    for load in loads:
        load.wait()

    def scale(i, carry):
        frow[rows(i * SUB), :] = frow[rows(i * SUB), :] * (1.0 / width)
        return carry

    lax.fori_loop(0, 8, scale, 0)

    def inner(first, last):
        def block(b, carry):
            at = rows(b * SUB)
            x = lax.dot_general(
                frow[...], fcol[at, :], (((1,), (1,)), ((), ())), preferred_element_type=F32
            )
            p = x * (3.0 + x * (3.0 + x))
            hi = p.astype(BF16)
            p_hi[:, at] = hi
            p_lo[:, at] = (p - hi.astype(F32)).astype(BF16)
            return carry

        lax.fori_loop(2 * first, 2 * last, block, 0)

    def product(at, cols, mem):
        both = jnp.dot(p_hi[at, cols], mem[cols, :], preferred_element_type=F32)
        low = jnp.dot(p_lo[at, cols], mem[cols, 0:clusters], preferred_element_type=F32)
        return both[:, :clusters] + both[:, clusters:] + low

    def first_pass(mem, actions):
        def chunk(i, carry):
            at = rows(i * 512, 512)
            total[at, :] = product(at, slice(0, 2048), mem)
            for step, action in actions:
                pl.when(i == step)(action)
            return carry

        lax.fori_loop(0, 4, chunk, 0)

    def exchange(members, buf, send, recv, group):
        buf[0] = jnp.broadcast_to(members, buf.shape[1:])
        copies = []
        for j, (where, slot) in enumerate(group):
            copies.append(
                pltpu.make_async_remote_copy(
                    src_ref=buf.at[0], dst_ref=buf.at[slot], send_sem=send.at[j],
                    recv_sem=recv.at[slot], device_id=where, device_id_type=MESH,
                )
            )
            copies[-1].start()

        def finish():
            for copy in copies:
                copy.wait_send()
            for _, slot in group:
                pltpu.make_async_copy(buf.at[slot], buf.at[slot], recv.at[slot]).wait()
            out = buf[0, 0:1, :]
            for _, slot in group:
                out = out + buf[slot, 0:1, :]
            return out

        return finish

    near_ids = [(device(dy=dy, dx2=dx), ((4 - dy) % 4) * 2 + dx) for dy, dx in reduce_group]
    far_ids = [
        (device(dz=dz, dx1=dx, dk=dk), ((4 - dz) % 4) * 4 + dx * 2 + dk) for dz, dx, dk in gather_group
    ]

    feats.forward_1()
    feats.forward_2()
    feats.forward_3()
    inner(0, 1)
    mems[0].forward_1()
    mems[0].forward_2()
    mems[0].forward_3()
    feats.wait(10, 11, 12)
    inner(1, 4)

    for it in range(ITERS):
        mem, stream = (mem0, mem1)[it], mems[it]
        if it == 0:
            feats.forward_45()
            feats.forward_6()
            stream.wait(9, 10, 11, 12)
            first_pass(
                mem,
                [(0, stream.forward_45), (1, feats.forward_7), (2, stream.forward_6), (3, stream.forward_7)],
            )
            feats.wait(13, 14)
            inner(4, 6)
            feats.wait(15, 16)
            inner(6, 8)
        else:
            stream.send_own()
            stream.forward_1()
            stream.forward_2()
            stream.forward_3()
            stream.wait(9, 10, 11, 12)
            first_pass(
                mem, [(1, stream.forward_45), (2, stream.forward_6), (3, stream.forward_7)]
            )
        stream.wait(13, 14, 15, 16)

        ones = jnp.ones((16, 8 * 2 * SUB), BF16)
        panel = jnp.dot(ones, mem[...], preferred_element_type=F32)[0:1]
        size_done = exchange(
            panel[:, :clusters] + panel[:, clusters:], vec.at[it, pl.ds(0, 8)],
            v_send.at[it, 0], v_recv.at[it, 0], near_ids,
        )

        rs = functools.partial(
            pltpu.make_async_remote_copy, device_id_type=MESH
        )
        sends = {}
        for j, dx in enumerate((1, 0)):
            u = j
            sends[u] = [
                rs(total.at[rows(u * SUB, 128)], mid.at[it, j, 0], r_send.at[it, 2 * j], r_recv.at[it, 2 * j], device_id=y_up),
                rs(total.at[rows(u * SUB + 128, 128)], mid.at[it, j, 1], r_send.at[it, 2 * j + 1], r_recv.at[it, 2 * j + 1], device_id=y_down),
            ]
            up, down = 2 + 2 * j, 3 + 2 * j
            sends[up] = [rs(total.at[rows(up * SUB)], near.at[it, j, 0], r_send.at[it, 4 + 2 * j], r_recv.at[it, 4 + 2 * j], device_id=y_up)]
            sends[down] = [rs(total.at[rows(down * SUB)], near.at[it, j, 1], r_send.at[it, 5 + 2 * j], r_recv.at[it, 5 + 2 * j], device_id=y_down)]
        sends[6] = [rs(total.at[rows(6 * SUB)], side.at[it], r_send.at[it, 8], r_recv.at[it, 8], device_id=across)]

        def ready(ref, n):
            pltpu.make_async_copy(ref, ref, r_recv.at[it, n]).wait()

        def after(u):
            def action():
                if 2 <= u <= 5:
                    j, half = (u - 2) // 2, u % 2
                    ready(mid.at[it, j, half], 2 * j + half)
                    at = rows(u * SUB + 128 * half, 128)
                    total[at, :] = total[at, :] + mid[it, j, half]
                if u >= 6:
                    j = u - 6
                    ready(near.at[it, j, 0], 4 + 2 * j)
                    ready(near.at[it, j, 1], 5 + 2 * j)
                    at = rows(u * SUB)
                    total[at, :] = total[at, :] + near[it, j, 0] + near[it, j, 1]
                for copy in sends.get(u, []):
                    copy.start()

            return action

        def step(u, carry):
            at = rows(u * SUB)
            total[at, :] = total[at, :] + product(at, slice(2048, 4096), mem)
            for v in range(8):
                pl.when(u == v)(after(v))
            return carry

        lax.fori_loop(0, 8, step, 0)
        size = size_done()
        ready(side.at[it], 8)
        for copies in sends.values():
            for copy in copies:
                copy.wait_send()
        scores = total[rows(7 * SUB), :] + side[it]
        members = own[...]
        weighted = exchange(
            jnp.sum(members * scores, axis=0, keepdims=True), vec.at[it, pl.ds(8, 8)],
            v_send.at[it, 1], v_recv.at[it, 1], near_ids,
        )()
        weighted = exchange(
            weighted, vec.at[it, pl.ds(16, 16)], v_send.at[it, 2], v_recv.at[it, 2], far_ids,
        )()
        distance = weighted / (size * size) - 2.0 * scores / size
        centered = distance - jnp.mean(distance, axis=1, keepdims=True)
        spread = jnp.mean(centered * centered, axis=1, keepdims=True)
        standardized = centered / jnp.sqrt(spread + 1e-06)
        members = softmax_rows(jnp.exp(-2.0 * standardized))
        if it + 1 < ITERS:
            put_members(members, mem1)
        else:
            memb_out[...] = members
            std_out[...] = standardized
        stream.finish()
    feats.finish()


def on_device(features, logits):
    frames, clusters = logits.shape
    width = features.shape[1]
    tall, wide = 8 * SUB, 16 * SUB
    vmem = pl.BlockSpec(memory_space=pltpu.VMEM)
    out = jax.ShapeDtypeStruct((frames, clusters), F32)
    dma = pltpu.SemaphoreType.DMA
    return pl.pallas_call(
        kernel,
        out_shape=(out, out),
        in_specs=[pl.BlockSpec(memory_space=pl.ANY), vmem],
        out_specs=(vmem, vmem),
        scratch_shapes=[
            pltpu.VMEM((tall, width), BF16),
            pltpu.VMEM((wide, width), BF16),
            pltpu.VMEM((wide, 2 * clusters), BF16),
            pltpu.VMEM((wide, 2 * clusters), BF16),
            pltpu.VMEM((tall, wide), BF16),
            pltpu.VMEM((tall, wide), BF16),
            pltpu.VMEM((SUB, clusters), F32),
            pltpu.VMEM((tall, clusters), F32),
            pltpu.VMEM((ITERS, 2, 2, 128, clusters), F32),
            pltpu.VMEM((ITERS, 2, 2, SUB, clusters), F32),
            pltpu.VMEM((ITERS, SUB, clusters), F32),
            pltpu.VMEM((ITERS, 32, 8, clusters), F32),
            dma((9,)),
            dma((24,)),
            dma((17,)),
            dma((ITERS, 24)),
            dma((ITERS, 17)),
            dma((ITERS, 9)),
            dma((ITERS, 9)),
            dma((ITERS, 3, 16)),
            dma((ITERS, 3, 16)),
        ],
        compiler_params=pltpu.CompilerParams(
            collective_id=0, has_side_effects=True, vmem_limit_bytes=62 * 1024 * 1024
        ),
    )(features, logits)


def solution(mesh):
    return jax.shard_map(
        on_device,
        mesh=mesh,
        in_specs=(P("row", None), P(("row", "col"), None)),
        out_specs=(P(("row", "col"), None), P(("row", "col"), None)),
        check_vma=False,
    )
```

```python
import jax
import jax.numpy as jnp
from jax import lax
from jax.experimental import pallas as pl
from jax.experimental.pallas import tpu as pltpu
from jax.sharding import PartitionSpec as P

ITERS = 2
SUB = 256
MESH = pl.DeviceIdType.MESH
BF16 = jnp.bfloat16
F32 = jnp.float32


def rows(start, size=SUB):
    return pl.ds(start if isinstance(start, int) else pl.multiple_of(start, 128), size)


def softmax_rows(raised):
    return raised / jnp.sum(raised, axis=1, keepdims=True)


def kernel(
    feat, logits, memb_out, std_out,
    frow, fcol, mem0, mem1, rows0, rows1, p_hi, p_lo, total, wsum,
    inbox, vec,
    load_sem, f_send, f_recv, m_send, m_recv, a_send, a_recv, r_send, r_recv, v_send, v_recv,
):
    clusters = logits.shape[1]
    width = feat.shape[1]
    row, col = lax.axis_index("row"), lax.axis_index("col")
    z, xh = row // 2, row % 2
    y, xl, core = col // 4, (col // 2) % 2, col % 2

    def device(dz=0, dx1=0, dy=0, dx2=0, dk=0):
        new_xh = (xh + dx1) % 2
        new_xl = (xl + dx1 + dx2) % 2
        return (
            ((z + dz) % 4) * 2 + new_xh,
            ((y + dy) % 4) * 4 + new_xl * 2 + (core + dk) % 2,
        )

    z_up, z_down, z_far = device(dz=1), device(dz=3), device(dz=2)
    cross, partner = device(dx1=1), device(dk=1)
    y_up, y_down, y_far, across = device(dy=1), device(dy=3), device(dy=2), device(dx2=1)
    reduce_group = [(dy, dx) for dy in range(4) for dx in range(2)][1:]
    gather_group = [(dz, dx, dk) for dz in range(4) for dx in range(2) for dk in range(2)][1:]

    barrier = pltpu.get_barrier_semaphore()
    nearest = (z_up, z_down, cross, partner, y_up, y_down, across)
    for where in nearest:
        pl.semaphore_signal(barrier, inc=1, device_id=where, device_id_type=MESH)

    order = [(2, 1), (2, 0), (1, 1), (3, 1), (1, 0), (3, 0), (0, 1), (0, 0)]
    loads = []
    for u, (dy, dx) in enumerate(order):
        block = ((y + dy) % 4) * 4 + ((xl + dx) % 2) * 2 + core
        loads.append(
            pltpu.make_async_copy(
                feat.at[rows(block * SUB)], frow.at[rows(u * SUB)], load_sem.at[u]
            )
        )
    loads.append(
        pltpu.make_async_copy(
            feat.at[rows((y * 4 + xl * 2) * SUB, 2 * SUB)], fcol.at[rows(0, 2 * SUB)], load_sem.at[8]
        )
    )
    for load in loads:
        load.start()

    def put_members(members, mem, tile_rows):
        hi = members.astype(BF16)
        lo = (members - hi.astype(F32)).astype(BF16)
        for ref, start in ((mem, core * SUB), (tile_rows, 7 * SUB)):
            ref[rows(start), 0:clusters] = hi
            ref[rows(start), clusters : 2 * clusters] = lo

    put_members(softmax_rows(jnp.exp(logits[...])), mem0, rows0)
    pl.semaphore_wait(barrier, len(nearest))

    class Stream:
        def __init__(self, buf, send, recv, own_src=None):
            self.buf, self.send, self.recv = buf, send, recv
            self.own_src = own_src
            self.sent = 0
            self.started = []

        def at(self, slot, half=None, other=False):
            part = 1 - core if other else core
            start = slot * 2 * SUB + part * SUB
            if half is None:
                return self.buf.at[rows(start)]
            return self.buf.at[rows(start + half * (SUB // 2), SUB // 2)]

        def make(self, src, dst, where, sem):
            n = self.sent
            self.sent += 1
            self.started.append((n, src))
            return pltpu.make_async_remote_copy(
                src_ref=src(), dst_ref=dst, send_sem=self.send.at[n], recv_sem=self.recv.at[sem],
                device_id=where, device_id_type=MESH,
            )

        def wait(self, *sems):
            for s in sems:
                if s >= 9:
                    dst = self.at(s - 9, other=True)
                elif s >= 8:
                    dst = self.at(7)
                elif s >= 6 and self.own_src is not None:
                    dst = self.at(6, s - 6)
                else:
                    dst = self.at(s)
                pltpu.make_async_copy(dst, dst, self.recv.at[s]).wait()

        def send_own(self):
            src = self.own_src or (lambda: self.at(0))
            self.make(src, self.at(2), z_up, 2).start()
            self.make(src, self.at(3), z_down, 3).start()
            self.make(src, self.at(1), cross, 1).start()
            if self.own_src is None:
                self.make(src, self.at(0), partner, 9).start()

        def to_partner(self, slot):
            self.make(lambda: self.at(slot), self.at(slot), partner, 9 + slot).start()

        def forward_1(self):
            self.wait(1)
            self.make(lambda: self.at(1), self.at(4), z_up, 4).start()
            self.make(lambda: self.at(1), self.at(5), z_down, 5).start()
            self.to_partner(1)

        def send_far(self):
            self.make(lambda: self.at(0), self.at(6), z_far, 6).start()

        def forward_2(self):
            self.wait(2)
            if self.own_src is not None:
                self.make(lambda: self.at(2, 0), self.at(6, 0), z_up, 6).start()
            self.to_partner(2)

        def forward_3(self):
            self.wait(3)
            if self.own_src is not None:
                self.make(lambda: self.at(3, 1), self.at(6, 1), z_down, 7).start()
            self.to_partner(3)

        def forward_45(self):
            self.wait(4)
            self.to_partner(4)
            self.wait(5)
            self.to_partner(5)

        def forward_6(self):
            self.wait(6)
            if self.own_src is not None:
                self.wait(7)
            self.make(lambda: self.at(6), self.at(7), cross, 8).start()
            self.to_partner(6)

        def forward_7(self):
            self.wait(8)
            self.to_partner(7)

        def finish(self):
            for n, src in self.started:
                pltpu.make_async_copy(src(), src(), self.send.at[n]).wait()

    feats = Stream(fcol, f_send, f_recv, lambda: feat.at[rows(col * SUB)])
    mems = [Stream(mem, m_send.at[i], m_recv.at[i]) for i, mem in enumerate((mem0, mem1))]

    def row_copy(it, dy, dx):
        there = order.index(((4 - dy) % 4, dx))
        buf = (rows0, rows1)[it]
        return pltpu.make_async_remote_copy(
            src_ref=buf.at[rows(7 * SUB)], dst_ref=buf.at[rows(there * SUB)],
            send_sem=a_send.at[it, there], recv_sem=a_recv.at[it, there],
            device_id=device(dy=dy, dx2=dx), device_id_type=MESH,
        )

    def send_rows(it, group):
        for dy, dx in group:
            row_copy(it, dy, dx).start()

    def wait_rows(it, group):
        for dy, dx in group:
            row_copy(it, (4 - dy) % 4, dx).wait_recv()

    row_near, row_mid, row_far = [(1, 0), (3, 0), (0, 1)], [(2, 0), (1, 1), (3, 1)], [(2, 1)]

    feats.send_own()
    mems[0].send_own()
    send_rows(0, row_near)

    for load in loads:
        load.wait()

    def scale(i, carry):
        frow[rows(i * SUB), :] = frow[rows(i * SUB), :] * (1.0 / width)
        return carry

    lax.fori_loop(0, 8, scale, 0)

    def inner(first, last):
        def block(b, carry):
            at = rows(b * SUB)
            x = lax.dot_general(
                frow[...], fcol[at, :], (((1,), (1,)), ((), ())), preferred_element_type=F32
            )
            p = x * (3.0 + x * (3.0 + x))
            hi = p.astype(BF16)
            p_hi[:, at] = hi
            p_lo[:, at] = (p - hi.astype(F32)).astype(BF16)
            return carry

        lax.fori_loop(2 * first, 2 * last, block, 0)

    def product(at, cols, mem):
        both = jnp.dot(p_hi[at, cols], mem[cols, :], preferred_element_type=F32)
        low = jnp.dot(p_lo[at, cols], mem[cols, 0:clusters], preferred_element_type=F32)
        return both[:, :clusters] + both[:, clusters:] + low

    def column_pass(mem, first, last, actions=()):
        def chunk(i, carry):
            at = rows(i * 512, 512)
            part = product(at, slice(first * 2 * SUB, last * 2 * SUB), mem)
            total[at, :] = part if first == 0 else total[at, :] + part
            for step, action in actions:
                pl.when(i == step)(action)
            return carry

        lax.fori_loop(0, 4, chunk, 0)

    def exchange(members, buf, send, recv, group):
        buf[0] = jnp.broadcast_to(members, buf.shape[1:])
        copies = []
        for j, (where, slot) in enumerate(group):
            copies.append(
                pltpu.make_async_remote_copy(
                    src_ref=buf.at[0], dst_ref=buf.at[slot], send_sem=send.at[j],
                    recv_sem=recv.at[slot], device_id=where, device_id_type=MESH,
                )
            )
            copies[-1].start()

        def finish():
            for copy in copies:
                copy.wait_send()
            for _, slot in group:
                pltpu.make_async_copy(buf.at[slot], buf.at[slot], recv.at[slot]).wait()
            out = buf[0, 0:1, :]
            for _, slot in group:
                out = out + buf[slot, 0:1, :]
            return out

        return finish

    near_ids = [(device(dy=dy, dx2=dx), ((4 - dy) % 4) * 2 + dx) for dy, dx in reduce_group]
    far_ids = [
        (device(dz=dz, dx1=dx, dk=dk), ((4 - dz) % 4) * 4 + dx * 2 + dk) for dz, dx, dk in gather_group
    ]

    for it in range(ITERS):
        mem, stream, tile_rows = (mem0, mem1)[it], mems[it], (rows0, rows1)[it]
        if it == 0:
            inner(0, 1)
            stream.wait(9)
            column_pass(mem, 0, 1)
            feats.forward_2()
            feats.forward_3()
            feats.forward_1()
            wait_rows(0, row_near)
            send_rows(0, row_mid)
            stream.send_far()
            stream.forward_1()
            feats.wait(10, 11, 12)
            inner(1, 2)
            stream.forward_2()
            stream.forward_3()
            wait_rows(0, row_mid)
            send_rows(0, row_far)
            inner(2, 3)
            feats.forward_6()
            inner(3, 4)
            stream.wait(10, 11, 12)
            column_pass(
                mem, 1, 4,
                [(0, feats.forward_45), (1, stream.forward_6), (2, stream.forward_45)],
            )
            feats.wait(13, 14)
            inner(4, 5)
            feats.forward_7()
            inner(5, 6)
            stream.forward_7()
            feats.wait(15, 16)
            inner(6, 8)
            wait_rows(0, row_far)
        else:
            stream.send_own()
            stream.send_far()
            send_rows(it, row_near + row_mid + row_far)
            stream.wait(9)
            column_pass(mem, 0, 1)
            stream.forward_1()
            stream.forward_2()
            stream.forward_3()
            stream.wait(10, 11, 12)
            column_pass(mem, 1, 4, [(2, stream.forward_6), (3, stream.forward_45)])
            wait_rows(it, row_near + row_mid + row_far)
        stream.wait(13, 14)
        column_pass(mem, 4, 6, [(3, stream.forward_7)] if it else ())
        stream.wait(15, 16)

        ones = jnp.ones((16, 8 * 2 * SUB), BF16)
        panel = jnp.dot(ones, mem[...], preferred_element_type=F32)[0:1]
        size_done = exchange(
            panel[:, :clusters] + panel[:, clusters:], vec.at[it, pl.ds(0, 8)],
            v_send.at[it, 0], v_recv.at[it, 0], near_ids,
        )

        def score_copy(u, slot, where):
            return pltpu.make_async_remote_copy(
                src_ref=total.at[rows(u * SUB)], dst_ref=inbox.at[it, slot],
                send_sem=r_send.at[it, slot], recv_sem=r_recv.at[it, slot],
                device_id=where, device_id_type=MESH,
            )

        routes = [
            (0, 0, across), (2, 1, y_up), (3, 2, y_down), (4, 3, y_up), (5, 4, y_down), (1, 5, y_far), (6, 6, across),
        ]
        wsum[...] = jnp.zeros_like(wsum)

        def step(u, carry):
            at = rows(u * SUB)
            part = total[at, :] + product(at, slice(6 * 2 * SUB, 8 * 2 * SUB), mem)
            total[at, :] = part
            weights = tile_rows[at, 0:clusters].astype(F32) + tile_rows[at, clusters : 2 * clusters].astype(F32)
            wsum[...] += jnp.sum((weights * part).reshape(SUB // 8, 8, clusters), axis=0)
            for v, slot, where in routes[:5]:
                pl.when(u == v)(lambda v=v, slot=slot, where=where: score_copy(v, slot, where).start())
            return carry

        lax.fori_loop(0, 8, step, 0)
        weighted_done = exchange(
            jnp.sum(wsum[...], axis=0, keepdims=True), vec.at[it, pl.ds(8, 8)],
            v_send.at[it, 1], v_recv.at[it, 1], near_ids,
        )
        score_copy(*routes[0]).wait_recv()
        total[rows(SUB), :] = total[rows(SUB), :] + inbox[it, 0]
        score_copy(*routes[5]).start()
        score_copy(*routes[1]).wait_recv()
        score_copy(*routes[2]).wait_recv()
        total[rows(6 * SUB), :] = total[rows(6 * SUB), :] + inbox[it, 1] + inbox[it, 2]
        score_copy(*routes[6]).start()
        weighted_done = exchange(
            weighted_done(), vec.at[it, pl.ds(16, 16)], v_send.at[it, 2], v_recv.at[it, 2], far_ids,
        )
        size = size_done()
        weighted = weighted_done()
        for route in routes[3:]:
            score_copy(*route).wait_recv()
        scores = total[rows(7 * SUB), :]
        for slot in range(3, 7):
            scores = scores + inbox[it, slot]
        distance = weighted / (size * size) - 2.0 * scores / size
        centered = distance - jnp.mean(distance, axis=1, keepdims=True)
        spread = jnp.mean(centered * centered, axis=1, keepdims=True)
        standardized = centered / jnp.sqrt(spread + 1e-06)
        members = softmax_rows(jnp.exp(-2.0 * standardized))
        for route in routes:
            score_copy(*route).wait_send()
        if it + 1 < ITERS:
            put_members(members, mem1, rows1)
        else:
            memb_out[...] = members
            std_out[...] = standardized
    for it in range(ITERS):
        mems[it].finish()
        for dy, dx in row_near + row_mid + row_far:
            row_copy(it, dy, dx).wait_send()
    feats.finish()


def on_device(features, logits):
    frames, clusters = logits.shape
    width = features.shape[1]
    tall, wide = 8 * SUB, 16 * SUB
    vmem = pl.BlockSpec(memory_space=pltpu.VMEM)
    out = jax.ShapeDtypeStruct((frames, clusters), F32)
    dma = pltpu.SemaphoreType.DMA
    return pl.pallas_call(
        kernel,
        out_shape=(out, out),
        in_specs=[pl.BlockSpec(memory_space=pl.ANY), vmem],
        out_specs=(vmem, vmem),
        scratch_shapes=[
            pltpu.VMEM((tall, width), BF16),
            pltpu.VMEM((wide, width), BF16),
            pltpu.VMEM((wide, 2 * clusters), BF16),
            pltpu.VMEM((wide, 2 * clusters), BF16),
            pltpu.VMEM((tall, 2 * clusters), BF16),
            pltpu.VMEM((tall, 2 * clusters), BF16),
            pltpu.VMEM((tall, wide), BF16),
            pltpu.VMEM((tall, wide), BF16),
            pltpu.VMEM((tall, clusters), F32),
            pltpu.VMEM((8, clusters), F32),
            pltpu.VMEM((ITERS, 7, SUB, clusters), F32),
            pltpu.VMEM((ITERS, 32, 8, clusters), F32),
            dma((9,)),
            dma((24,)),
            dma((17,)),
            dma((ITERS, 24)),
            dma((ITERS, 17)),
            dma((ITERS, 7)),
            dma((ITERS, 7)),
            dma((ITERS, 7)),
            dma((ITERS, 7)),
            dma((ITERS, 3, 16)),
            dma((ITERS, 3, 16)),
        ],
        compiler_params=pltpu.CompilerParams(
            collective_id=0, has_side_effects=True, vmem_limit_bytes=62 * 1024 * 1024
        ),
    )(features, logits)


def solution(mesh):
    return jax.shard_map(
        on_device,
        mesh=mesh,
        in_specs=(P("row", None), P(("row", "col"), None)),
        out_specs=(P(("row", "col"), None), P(("row", "col"), None)),
        check_vma=False,
    )
```

```python
import jax
import jax.numpy as jnp
from jax import lax
from jax.experimental import pallas as pl
from jax.experimental.pallas import tpu as pltpu
from jax.sharding import PartitionSpec as P

ITERS = 2
SUB = 256
MESH = pl.DeviceIdType.MESH
BF16 = jnp.bfloat16
F32 = jnp.float32


def rows(start, size=SUB):
    return pl.ds(start if isinstance(start, int) else pl.multiple_of(start, 128), size)


def softmax_rows(raised):
    return raised / jnp.sum(raised, axis=1, keepdims=True)


def kernel(
    feat, logits, memb_out, std_out,
    frow, fcol, mem0, mem1, rows0, rows1, p_hi, p_lo, total, wsum,
    inbox, vec,
    load_sem, f_send, f_recv, m_send, m_recv, a_send, a_recv, r_send, r_recv, v_send, v_recv,
):
    clusters = logits.shape[1]
    width = feat.shape[1]
    row, col = lax.axis_index("row"), lax.axis_index("col")
    z, xh = row // 2, row % 2
    y, xl, core = col // 4, (col // 2) % 2, col % 2

    def device(dz=0, dx1=0, dy=0, dx2=0, dk=0):
        new_xh = (xh + dx1) % 2
        new_xl = (xl + dx1 + dx2) % 2
        return (
            ((z + dz) % 4) * 2 + new_xh,
            ((y + dy) % 4) * 4 + new_xl * 2 + (core + dk) % 2,
        )

    z_up, z_down, z_far = device(dz=1), device(dz=3), device(dz=2)
    cross, partner = device(dx1=1), device(dk=1)
    y_up, y_down, y_far, across = device(dy=1), device(dy=3), device(dy=2), device(dx2=1)
    reduce_group = [(dy, dx) for dy in range(4) for dx in range(2)][1:]
    gather_group = [(dz, dx, dk) for dz in range(4) for dx in range(2) for dk in range(2)][1:]

    barrier = pltpu.get_barrier_semaphore()
    nearest = (z_up, z_down, cross, partner, y_up, y_down, across)
    for where in nearest:
        pl.semaphore_signal(barrier, inc=1, device_id=where, device_id_type=MESH)

    order = [(2, 1), (2, 0), (1, 1), (3, 1), (1, 0), (3, 0), (0, 1), (0, 0)]
    loads = []
    for u, (dy, dx) in enumerate(order):
        block = ((y + dy) % 4) * 4 + ((xl + dx) % 2) * 2 + core
        loads.append(
            pltpu.make_async_copy(
                feat.at[rows(block * SUB)], frow.at[rows(u * SUB)], load_sem.at[u]
            )
        )
    loads.append(
        pltpu.make_async_copy(
            feat.at[rows((y * 4 + xl * 2) * SUB, 2 * SUB)], fcol.at[rows(0, 2 * SUB)], load_sem.at[8]
        )
    )
    for load in loads:
        load.start()

    def put_members(members, mem, tile_rows):
        hi = members.astype(BF16)
        lo = (members - hi.astype(F32)).astype(BF16)
        for ref, start in ((mem, core * SUB), (tile_rows, 7 * SUB)):
            ref[rows(start), 0:clusters] = hi
            ref[rows(start), clusters : 2 * clusters] = lo

    put_members(softmax_rows(jnp.exp(logits[...])), mem0, rows0)
    pl.semaphore_wait(barrier, len(nearest))

    class Stream:
        def __init__(self, buf, send, recv, own_src=None):
            self.buf, self.send, self.recv, self.own_src = buf, send, recv, own_src
            self.started = []

        def at(self, slot, half=None, other=False):
            start = slot * 2 * SUB + (1 - core if other else core) * SUB
            if half is None:
                return self.buf.at[rows(start)]
            return self.buf.at[rows(start + half * (SUB // 2), SUB // 2)]

        def own(self, half=None):
            if self.own_src is None:
                return self.at(0, half)
            start = self.own_src[1]
            if half is None:
                return self.own_src[0].at[rows(start)]
            return self.own_src[0].at[rows(start + half * (SUB // 2), SUB // 2)]

        def put(self, src, slot, where, half=None):
            n = len(self.started)
            self.started.append(src)
            sem = 16 + slot if where is partner else 2 * slot + (half or 0)
            pltpu.make_async_remote_copy(
                src_ref=src(), dst_ref=self.at(slot, half), send_sem=self.send.at[n],
                recv_sem=self.recv.at[sem], device_id=where, device_id_type=MESH,
            ).start()

        def wait(self, slot, half=None):
            dst = self.at(slot, half)
            pltpu.make_async_copy(dst, dst, self.recv.at[2 * slot + (half or 0)]).wait()

        def ready(self, *slots):
            for slot in slots:
                dst = self.at(slot, other=True)
                pltpu.make_async_copy(dst, dst, self.recv.at[16 + slot]).wait()

        def pass_on(self, slot, *where):
            for there, device_id in where:
                self.put(lambda: self.at(slot), there, device_id)
            self.put(lambda: self.at(slot), slot, partner)

        def relay(self, *slots):
            for slot in slots:
                self.wait(slot)
                if slot == 1:
                    self.pass_on(1, (5, z_up), (6, z_down))
                elif slot == 2:
                    self.pass_on(2, (7, cross))
                else:
                    self.pass_on(slot)

        def finish(self):
            for n, src in enumerate(self.started):
                pltpu.make_async_copy(src(), src(), self.send.at[n]).wait()

    feats = Stream(fcol, f_send, f_recv, (feat, col * SUB))
    mems = [Stream(mem, m_send.at[i], m_recv.at[i]) for i, mem in enumerate((mem0, mem1))]

    def row_copy(it, dy, dx):
        there = order.index(((4 - dy) % 4, dx))
        buf = (rows0, rows1)[it]
        return pltpu.make_async_remote_copy(
            src_ref=buf.at[rows(7 * SUB)], dst_ref=buf.at[rows(there * SUB)],
            send_sem=a_send.at[it, there], recv_sem=a_recv.at[it, there],
            device_id=device(dy=dy, dx2=dx), device_id_type=MESH,
        )

    def send_rows(it, group):
        for dy, dx in group:
            row_copy(it, dy, dx).start()

    def wait_rows(it, group):
        for dy, dx in group:
            row_copy(it, (4 - dy) % 4, dx).wait_recv()

    row_near, row_mid, row_far = [(1, 0), (3, 0), (0, 1)], [(2, 0), (1, 1), (3, 1)], [(2, 1)]

    for first in range(2):
        feats.put(lambda h=first: feats.own(h), 3, z_up, first)
        feats.put(lambda h=1 - first: feats.own(h), 4, z_down, 1 - first)
    feats.put(feats.own, 1, cross)
    mems[0].put(mems[0].own, 0, partner)
    mems[0].put(mems[0].own, 1, cross)
    send_rows(0, row_near)

    for load in loads:
        load.wait()

    def scale(i, carry):
        frow[rows(i * SUB), :] = frow[rows(i * SUB), :] * (1.0 / width)
        return carry

    lax.fori_loop(0, 8, scale, 0)

    def inner(first, last):
        def block(b, carry):
            at = rows(b * SUB)
            x = lax.dot_general(
                frow[...], fcol[at, :], (((1,), (1,)), ((), ())), preferred_element_type=F32
            )
            p = x * (3.0 + x * (3.0 + x))
            hi = p.astype(BF16)
            p_hi[:, at] = hi
            p_lo[:, at] = (p - hi.astype(F32)).astype(BF16)
            return carry

        lax.fori_loop(2 * first, 2 * last, block, 0)

    def product(at, cols, mem):
        both = jnp.dot(p_hi[at, cols], mem[cols, :], preferred_element_type=F32)
        low = jnp.dot(p_lo[at, cols], mem[cols, 0:clusters], preferred_element_type=F32)
        return both[:, :clusters] + both[:, clusters:] + low

    def column_pass(mem, first, last, actions=()):
        def chunk(i, carry):
            at = rows(i * 512, 512)
            part = product(at, slice(first * 2 * SUB, last * 2 * SUB), mem)
            total[at, :] = part if first == 0 else total[at, :] + part
            for step, action in actions:
                pl.when(i == step)(action)
            return carry

        lax.fori_loop(0, 4, chunk, 0)

    def exchange(values, buf, send, recv, group):
        buf[0] = values
        copies = [
            pltpu.make_async_remote_copy(
                src_ref=buf.at[0], dst_ref=buf.at[slot], send_sem=send.at[slot],
                recv_sem=recv.at[slot], device_id=where, device_id_type=MESH,
            )
            for where, slot in group
        ]
        for copy in copies:
            copy.start()

        def finish():
            out = buf[0]
            for copy, (_, slot) in zip(copies, group):
                pltpu.make_async_copy(buf.at[slot], buf.at[slot], recv.at[slot]).wait()
                copy.wait_send()
                out = out + buf[slot]
            return out

        return finish

    near_ids = [(device(dy=dy, dx2=dx), ((4 - dy) % 4) * 2 + dx) for dy, dx in reduce_group]
    far_ids = [
        (device(dz=dz, dx1=dx, dk=dk), ((4 - dz) % 4) * 4 + dx * 2 + dk) for dz, dx, dk in gather_group
    ]

    for it in range(ITERS):
        mem, stream, tile_rows = (mem0, mem1)[it], mems[it], (rows0, rows1)[it]
        row_all = row_near + row_mid + row_far
        if it == 0:
            inner(0, 1)
            stream.ready(0)
            column_pass(mem, 0, 1)
            feats.wait(3, 0)
            feats.put(lambda: feats.at(3, 0), 2, z_up, 0)
            feats.wait(4, 1)
            feats.put(lambda: feats.at(4, 1), 2, z_down, 1)
            stream.put(stream.own, 2, z_far)
            stream.put(stream.own, 3, z_up)
            stream.put(stream.own, 4, z_down)
            feats.relay(1)
            for slot, half in ((3, 1), (4, 0)):
                feats.wait(slot, half)
                feats.pass_on(slot)
            wait_rows(0, row_near)
            send_rows(0, row_mid)
            feats.ready(1)
            inner(1, 2)
            feats.wait(2, 0)
            feats.wait(2, 1)
            feats.pass_on(2, (7, cross))
            stream.relay(1)
            feats.ready(3, 4)
            inner(3, 5)
            wait_rows(0, row_mid)
            send_rows(0, row_far)
            stream.relay(2)
            feats.ready(2)
            inner(2, 3)
            stream.relay(3, 4)
            stream.ready(1, 2)
            column_pass(mem, 1, 3, [(3, lambda: feats.relay(7))])
            stream.ready(3, 4)
            column_pass(mem, 3, 5, [(2, lambda: feats.relay(5, 6))])
            feats.ready(7)
            inner(7, 8)
            feats.ready(5, 6)
            inner(5, 6)
            stream.relay(7)
            inner(6, 7)
            stream.relay(5, 6)
        else:
            stream.put(stream.own, 0, partner)
            stream.put(stream.own, 2, z_far)
            stream.put(stream.own, 1, cross)
            stream.put(stream.own, 3, z_up)
            stream.put(stream.own, 4, z_down)
            send_rows(it, row_all)
            stream.ready(0)
            column_pass(mem, 0, 1)
            stream.relay(1)
            stream.ready(1)
            column_pass(mem, 1, 2)
            stream.relay(2, 3, 4)
            stream.ready(2, 3, 4)
            column_pass(mem, 2, 5, [(1, lambda: stream.relay(5, 6)), (3, lambda: stream.relay(7))])
        stream.ready(5, 6, 7)

        def score_copy(u, slot, where):
            return pltpu.make_async_remote_copy(
                src_ref=total.at[rows(u * SUB)], dst_ref=inbox.at[it, slot],
                send_sem=r_send.at[it, slot], recv_sem=r_recv.at[it, slot],
                device_id=where, device_id_type=MESH,
            )

        routes = [
            (0, 0, across), (2, 1, y_up), (3, 2, y_down), (4, 3, y_up), (5, 4, y_down), (1, 5, y_far), (6, 6, across),
        ]
        def of(ref, at):
            return ref[at, 0:clusters].astype(F32) + ref[at, clusters : 2 * clusters].astype(F32)

        def fold(values):
            return jnp.sum(values.reshape(SUB // 8, 8, clusters), axis=0)

        wait_rows(it, row_far if it == 0 else row_all)
        wsum[...] = jnp.zeros_like(wsum)

        def step(u, carry):
            at = rows(u * SUB)
            part = total[at, :] + product(at, slice(5 * 2 * SUB, 8 * 2 * SUB), mem)
            total[at, :] = part
            wsum[...] += fold(of(tile_rows, at) * part)
            for v, slot, where in routes[:5]:
                pl.when(u == v)(lambda v=v, slot=slot, where=where: score_copy(v, slot, where).start())
            return carry

        lax.fori_loop(0, 8, step, 0)
        sizes = fold(of(tile_rows, rows(7 * SUB)))
        first = lax.broadcasted_iota(jnp.int32, (8, clusters), 0) == 0
        sums_done = exchange(
            jnp.where(
                first, jnp.sum(wsum[...], axis=0, keepdims=True), jnp.sum(sizes, axis=0, keepdims=True)
            ),
            vec.at[it, pl.ds(0, 16)], v_send.at[it, 0], v_recv.at[it, 0], far_ids,
        )
        score_copy(*routes[0]).wait_recv()
        total[rows(SUB), :] = total[rows(SUB), :] + inbox[it, 0]
        score_copy(*routes[5]).start()
        sums_done = exchange(
            sums_done(), vec.at[it, pl.ds(16, 8)], v_send.at[it, 1], v_recv.at[it, 1], near_ids,
        )
        score_copy(*routes[1]).wait_recv()
        score_copy(*routes[2]).wait_recv()
        total[rows(6 * SUB), :] = total[rows(6 * SUB), :] + inbox[it, 1] + inbox[it, 2]
        score_copy(*routes[6]).start()
        sums = sums_done()
        weighted, size = sums[0:1], sums[1:2]
        for route in routes[3:]:
            score_copy(*route).wait_recv()
        scores = total[rows(7 * SUB), :]
        for slot in range(3, 7):
            scores = scores + inbox[it, slot]
        distance = weighted / (size * size) - 2.0 * scores / size
        centered = distance - jnp.mean(distance, axis=1, keepdims=True)
        spread = jnp.mean(centered * centered, axis=1, keepdims=True)
        standardized = centered / jnp.sqrt(spread + 1e-06)
        members = softmax_rows(jnp.exp(-2.0 * standardized))
        for route in routes:
            score_copy(*route).wait_send()
        if it + 1 < ITERS:
            put_members(members, mem1, rows1)
        else:
            memb_out[...] = members
            std_out[...] = standardized
    for it in range(ITERS):
        mems[it].finish()
        for dy, dx in row_near + row_mid + row_far:
            row_copy(it, dy, dx).wait_send()
    feats.finish()


def on_device(features, logits):
    frames, clusters = logits.shape
    width = features.shape[1]
    tall, wide = 8 * SUB, 16 * SUB
    vmem = pl.BlockSpec(memory_space=pltpu.VMEM)
    out = jax.ShapeDtypeStruct((frames, clusters), F32)
    dma = pltpu.SemaphoreType.DMA
    return pl.pallas_call(
        kernel,
        out_shape=(out, out),
        in_specs=[pl.BlockSpec(memory_space=pl.ANY), vmem],
        out_specs=(vmem, vmem),
        scratch_shapes=[
            pltpu.VMEM((tall, width), BF16),
            pltpu.VMEM((wide, width), BF16),
            pltpu.VMEM((wide, 2 * clusters), BF16),
            pltpu.VMEM((wide, 2 * clusters), BF16),
            pltpu.VMEM((tall, 2 * clusters), BF16),
            pltpu.VMEM((tall, 2 * clusters), BF16),
            pltpu.VMEM((tall, wide), BF16),
            pltpu.VMEM((tall, wide), BF16),
            pltpu.VMEM((tall, clusters), F32),
            pltpu.VMEM((8, clusters), F32),
            pltpu.VMEM((ITERS, 7, SUB, clusters), F32),
            pltpu.VMEM((ITERS, 24, 8, clusters), F32),
            dma((9,)),
            dma((24,)),
            dma((24,)),
            dma((ITERS, 24)),
            dma((ITERS, 24)),
            dma((ITERS, 7)),
            dma((ITERS, 7)),
            dma((ITERS, 7)),
            dma((ITERS, 7)),
            dma((ITERS, 2, 16)),
            dma((ITERS, 2, 16)),
        ],
        compiler_params=pltpu.CompilerParams(
            collective_id=0, has_side_effects=True, vmem_limit_bytes=62 * 1024 * 1024
        ),
    )(features, logits)


def solution(mesh):
    return jax.shard_map(
        on_device,
        mesh=mesh,
        in_specs=(P("row", None), P(("row", "col"), None)),
        out_specs=(P(("row", "col"), None), P(("row", "col"), None)),
        check_vma=False,
    )
```

```python
import jax
import jax.numpy as jnp
from jax import lax
from jax.experimental import pallas as pl
from jax.experimental.pallas import tpu as pltpu
from jax.sharding import PartitionSpec as P

ITERS = 2
SUB = 256
MESH = pl.DeviceIdType.MESH
BF16 = jnp.bfloat16
F32 = jnp.float32


def rows(start, size=SUB):
    return pl.ds(start if isinstance(start, int) else pl.multiple_of(start, 128), size)


def softmax_rows(raised):
    return raised / jnp.sum(raised, axis=1, keepdims=True)


def kernel(
    feat, logits, memb_out, std_out,
    frow, fcol, mem0, mem1, rows0, rows1, p_hi, p_lo, total, wsum,
    inbox, vec,
    load_sem, f_send, f_recv, m_send, m_recv, a_send, a_recv, r_send, r_recv, v_send, v_recv,
):
    clusters = logits.shape[1]
    width = feat.shape[1]
    row, col = lax.axis_index("row"), lax.axis_index("col")
    z, xh = row // 2, row % 2
    y, xl, core = col // 4, (col // 2) % 2, col % 2

    def device(dz=0, dx1=0, dy=0, dx2=0, dk=0):
        new_xh = (xh + dx1) % 2
        new_xl = (xl + dx1 + dx2) % 2
        return (
            ((z + dz) % 4) * 2 + new_xh,
            ((y + dy) % 4) * 4 + new_xl * 2 + (core + dk) % 2,
        )

    z_up, z_down, z_far = device(dz=1), device(dz=3), device(dz=2)
    cross, partner = device(dx1=1), device(dk=1)
    y_up, y_down, y_far, across = device(dy=1), device(dy=3), device(dy=2), device(dx2=1)
    reduce_group = [(dy, dx) for dy in range(4) for dx in range(2)][1:]
    gather_group = [(dz, dx, dk) for dz in range(4) for dx in range(2) for dk in range(2)][1:]

    barrier = pltpu.get_barrier_semaphore()
    nearest = (z_up, z_down, cross, partner, y_up, y_down, across)
    for where in nearest:
        pl.semaphore_signal(barrier, inc=1, device_id=where, device_id_type=MESH)

    order = [(2, 1), (1, 1), (3, 1), (1, 0), (3, 0), (2, 0), (0, 1), (0, 0)]
    loads = []
    for u, (dy, dx) in enumerate(order):
        block = ((y + dy) % 4) * 4 + ((xl + dx) % 2) * 2 + core
        loads.append(
            pltpu.make_async_copy(
                feat.at[rows(block * SUB)], frow.at[rows(u * SUB)], load_sem.at[u]
            )
        )
    loads.append(
        pltpu.make_async_copy(
            feat.at[rows((y * 4 + xl * 2) * SUB, 2 * SUB)], fcol.at[rows(0, 2 * SUB)], load_sem.at[8]
        )
    )
    for load in loads:
        load.start()

    def put_members(members, mem, tile_rows):
        hi = members.astype(BF16)
        lo = (members - hi.astype(F32)).astype(BF16)
        for ref, start in ((mem, core * SUB), (tile_rows, 7 * SUB)):
            ref[rows(start), 0:clusters] = hi
            ref[rows(start), clusters : 2 * clusters] = lo

    put_members(softmax_rows(jnp.exp(logits[...])), mem0, rows0)
    pl.semaphore_wait(barrier, len(nearest))

    class Stream:
        def __init__(self, buf, send, recv, halves, own_src=None):
            self.buf, self.send, self.recv, self.own_src = buf, send, recv, own_src
            self.halves = halves
            self.started = []

        def at(self, slot, half=None, other=False):
            start = slot * 2 * SUB + (1 - core if other else core) * SUB
            if half is None:
                return self.buf.at[rows(start)]
            return self.buf.at[rows(start + half * (SUB // 2), SUB // 2)]

        def own(self, half=None):
            if self.own_src is None:
                return self.at(0, half)
            start = self.own_src[1]
            if half is None:
                return self.own_src[0].at[rows(start)]
            return self.own_src[0].at[rows(start + half * (SUB // 2), SUB // 2)]

        def put(self, src, slot, where, half=None):
            n = len(self.started)
            self.started.append(src)
            sem = 16 + slot if where is partner else 2 * slot + (half or 0)
            pltpu.make_async_remote_copy(
                src_ref=src(), dst_ref=self.at(slot, half), send_sem=self.send.at[n],
                recv_sem=self.recv.at[sem], device_id=where, device_id_type=MESH,
            ).start()

        def wait(self, slot, half=None):
            dst = self.at(slot, half)
            pltpu.make_async_copy(dst, dst, self.recv.at[2 * slot + (half or 0)]).wait()

        def ready(self, *slots):
            for slot in slots:
                dst = self.at(slot, other=True)
                pltpu.make_async_copy(dst, dst, self.recv.at[16 + slot]).wait()

        def send_round(self):
            for first in range(2):
                self.put(lambda h=first: self.own(h), 3, z_up, first)
                self.put(lambda h=1 - first: self.own(h), 4, z_down, 1 - first)

        def ring(self):
            for slot, half, where in ((3, 0, z_up), (4, 1, z_down)):
                self.wait(slot, half)
                self.put(lambda slot=slot, half=half: self.at(slot, half), 2, where, half)

        def pass_on(self, slot, *where):
            for there, device_id in where:
                self.put(lambda: self.at(slot), there, device_id)
            self.put(lambda: self.at(slot), slot, partner)

        def relay(self, *slots):
            for slot in slots:
                if self.halves and slot == 2:
                    self.wait(2, 0)
                self.wait(slot, {2: 1, 3: 1, 4: 0}.get(slot) if self.halves else None)
                if slot == 1:
                    self.pass_on(1, (5, z_up), (6, z_down))
                elif slot == 2:
                    self.pass_on(2, (7, cross))
                else:
                    self.pass_on(slot)

        def finish(self):
            for n, src in enumerate(self.started):
                pltpu.make_async_copy(src(), src(), self.send.at[n]).wait()

    feats = Stream(fcol, f_send, f_recv, True, (feat, col * SUB))
    mems = [Stream(mem, m_send.at[i], m_recv.at[i], i == 1) for i, mem in enumerate((mem0, mem1))]

    def row_copy(it, dy, dx):
        there = order.index(((4 - dy) % 4, dx))
        buf = (rows0, rows1)[it]
        return pltpu.make_async_remote_copy(
            src_ref=buf.at[rows(7 * SUB)], dst_ref=buf.at[rows(there * SUB)],
            send_sem=a_send.at[it, there], recv_sem=a_recv.at[it, there],
            device_id=device(dy=dy, dx2=dx), device_id_type=MESH,
        )

    def send_rows(it, group):
        for dy, dx in group:
            row_copy(it, dy, dx).start()

    def wait_rows(it, group):
        for dy, dx in group:
            row_copy(it, (4 - dy) % 4, dx).wait_recv()

    row_near, row_mid, row_far = [(1, 0), (3, 0), (0, 1)], [(2, 0), (1, 1), (3, 1)], [(2, 1)]

    feats.send_round()
    feats.put(feats.own, 1, cross)
    mems[0].put(mems[0].own, 0, partner)
    mems[0].put(mems[0].own, 1, cross)
    send_rows(0, row_near)

    for load in loads:
        load.wait()

    def scale(i, carry):
        frow[rows(i * SUB), :] = frow[rows(i * SUB), :] * (1.0 / width)
        return carry

    lax.fori_loop(0, 8, scale, 0)

    def inner(first, last):
        def block(b, carry):
            at = rows(b * SUB)
            x = lax.dot_general(
                frow[...], fcol[at, :], (((1,), (1,)), ((), ())), preferred_element_type=F32
            )
            p = x * (3.0 + x * (3.0 + x))
            hi = p.astype(BF16)
            p_hi[:, at] = hi
            p_lo[:, at] = (p - hi.astype(F32)).astype(BF16)
            return carry

        lax.fori_loop(2 * first, 2 * last, block, 0)

    def product(at, cols, mem):
        both = jnp.dot(p_hi[at, cols], mem[cols, :], preferred_element_type=F32)
        low = jnp.dot(p_lo[at, cols], mem[cols, 0:clusters], preferred_element_type=F32)
        return both[:, :clusters] + both[:, clusters:] + low

    def column_pass(mem, first, last, actions=()):
        def chunk(i, carry):
            at = rows(i * 512, 512)
            part = product(at, slice(first * 2 * SUB, last * 2 * SUB), mem)
            total[at, :] = part if first == 0 else total[at, :] + part
            for step, action in actions:
                pl.when(i == step)(action)
            return carry

        lax.fori_loop(0, 4, chunk, 0)

    def exchange(values, buf, send, recv, group):
        buf[0] = values
        copies = [
            pltpu.make_async_remote_copy(
                src_ref=buf.at[0], dst_ref=buf.at[slot], send_sem=send.at[slot],
                recv_sem=recv.at[slot], device_id=where, device_id_type=MESH,
            )
            for where, slot in group
        ]
        for copy in copies:
            copy.start()

        def finish():
            out = buf[0]
            for copy, (_, slot) in zip(copies, group):
                pltpu.make_async_copy(buf.at[slot], buf.at[slot], recv.at[slot]).wait()
                copy.wait_send()
                out = out + buf[slot]
            return out

        return finish

    near_ids = [(device(dy=dy, dx2=dx), ((4 - dy) % 4) * 2 + dx) for dy, dx in reduce_group]
    far_ids = [
        (device(dz=dz, dx1=dx, dk=dk), ((4 - dz) % 4) * 4 + dx * 2 + dk) for dz, dx, dk in gather_group
    ]

    for it in range(ITERS):
        mem, stream, tile_rows = (mem0, mem1)[it], mems[it], (rows0, rows1)[it]
        row_all = row_near + row_mid + row_far
        if it == 0:
            inner(0, 1)
            stream.ready(0)
            column_pass(mem, 0, 1)
            feats.ring()
            stream.put(stream.own, 3, z_up)
            stream.put(stream.own, 4, z_down)
            stream.put(stream.own, 2, z_far)
            feats.relay(1, 3, 4)
            wait_rows(0, row_near)
            send_rows(0, row_mid)
            feats.ready(1)
            inner(1, 2)
            feats.relay(2)
            stream.relay(1)
            feats.ready(3, 4)
            inner(3, 5)
            wait_rows(0, row_mid)
            send_rows(0, row_far)
            stream.relay(2)
            feats.ready(2)
            inner(2, 3)
            stream.relay(3, 4)
            stream.ready(1, 2)
            column_pass(mem, 1, 3, [(3, lambda: feats.relay(7))])
            stream.ready(3, 4)
            column_pass(mem, 3, 5, [(1, lambda: feats.relay(5, 6)), (3, lambda: stream.relay(7))])
            feats.ready(7)
            inner(7, 8)
            stream.relay(5, 6)
            feats.ready(5, 6)
            inner(5, 7)
        else:
            stream.put(stream.own, 0, partner)
            stream.send_round()
            stream.put(stream.own, 1, cross)
            send_rows(it, row_all)
            stream.ready(0)
            column_pass(mem, 0, 1)
            stream.ring()
            stream.relay(1, 3, 4, 2)
            stream.ready(1)
            column_pass(mem, 1, 2)
            stream.ready(2, 3, 4)
            column_pass(mem, 2, 5, [(1, lambda: stream.relay(5, 6)), (2, lambda: stream.relay(7))])
        stream.ready(5, 6, 7)

        def score_copy(n):
            u, slot, start, size, where = routes[n]
            return pltpu.make_async_remote_copy(
                src_ref=total.at[rows(u * SUB + start, size)], dst_ref=inbox.at[it, slot, pl.ds(start, size)],
                send_sem=r_send.at[it, n], recv_sem=r_recv.at[it, n],
                device_id=where, device_id_type=MESH,
            )

        half = SUB // 2
        routes = [
            (0, 0, 0, SUB, across), (1, 1, 0, SUB, y_up), (2, 2, 0, SUB, y_down),
            (3, 3, 0, half, y_up), (4, 4, 0, half, y_down), (5, 5, 0, SUB, y_far), (6, 6, 0, SUB, across),
            (3, 3, half, half, y_up), (4, 4, half, half, y_down),
        ]

        def of(ref, at):
            return ref[at, 0:clusters].astype(F32) + ref[at, clusters : 2 * clusters].astype(F32)

        def fold(values):
            return jnp.sum(values.reshape(SUB // 8, 8, clusters), axis=0)

        wait_rows(it, row_far if it == 0 else row_all)
        wsum[...] = jnp.zeros_like(wsum)

        def step(u, carry):
            at = rows(u * SUB)
            part = total[at, :] + product(at, slice(5 * 2 * SUB, 8 * 2 * SUB), mem)
            total[at, :] = part
            wsum[...] += fold(of(tile_rows, at) * part)
            for v in range(5):
                pl.when(u == v)(lambda v=v: score_copy(v).start())
            return carry

        lax.fori_loop(0, 8, step, 0)
        sizes = fold(of(tile_rows, rows(7 * SUB)))
        first = lax.broadcasted_iota(jnp.int32, (8, clusters), 0) == 0
        sums_done = exchange(
            jnp.where(
                first, jnp.sum(wsum[...], axis=0, keepdims=True), jnp.sum(sizes, axis=0, keepdims=True)
            ),
            vec.at[it, pl.ds(0, 16)], v_send.at[it, 0], v_recv.at[it, 0], far_ids,
        )
        score_copy(0).wait_recv()
        total[rows(5 * SUB), :] = total[rows(5 * SUB), :] + inbox[it, 0]
        score_copy(5).start()
        score_copy(1).wait_recv()
        score_copy(2).wait_recv()
        total[rows(6 * SUB), :] = total[rows(6 * SUB), :] + inbox[it, 1] + inbox[it, 2]
        score_copy(6).start()
        score_copy(7).start()
        score_copy(8).start()
        sums_done = exchange(
            sums_done(), vec.at[it, pl.ds(16, 8)], v_send.at[it, 1], v_recv.at[it, 1], near_ids,
        )
        sums = sums_done()
        weighted, size = sums[0:1], sums[1:2]
        for n in range(3, 9):
            score_copy(n).wait_recv()
        scores = total[rows(7 * SUB), :]
        for slot in range(3, 7):
            scores = scores + inbox[it, slot]
        distance = weighted / (size * size) - 2.0 * scores / size
        centered = distance - jnp.mean(distance, axis=1, keepdims=True)
        spread = jnp.mean(centered * centered, axis=1, keepdims=True)
        standardized = centered / jnp.sqrt(spread + 1e-06)
        members = softmax_rows(jnp.exp(-2.0 * standardized))
        for n in range(9):
            score_copy(n).wait_send()
        if it + 1 < ITERS:
            put_members(members, mem1, rows1)
        else:
            memb_out[...] = members
            std_out[...] = standardized
    for it in range(ITERS):
        mems[it].finish()
        for dy, dx in row_near + row_mid + row_far:
            row_copy(it, dy, dx).wait_send()
    feats.finish()


def on_device(features, logits):
    frames, clusters = logits.shape
    width = features.shape[1]
    tall, wide = 8 * SUB, 16 * SUB
    vmem = pl.BlockSpec(memory_space=pltpu.VMEM)
    out = jax.ShapeDtypeStruct((frames, clusters), F32)
    dma = pltpu.SemaphoreType.DMA
    return pl.pallas_call(
        kernel,
        out_shape=(out, out),
        in_specs=[pl.BlockSpec(memory_space=pl.ANY), vmem],
        out_specs=(vmem, vmem),
        scratch_shapes=[
            pltpu.VMEM((tall, width), BF16),
            pltpu.VMEM((wide, width), BF16),
            pltpu.VMEM((wide, 2 * clusters), BF16),
            pltpu.VMEM((wide, 2 * clusters), BF16),
            pltpu.VMEM((tall, 2 * clusters), BF16),
            pltpu.VMEM((tall, 2 * clusters), BF16),
            pltpu.VMEM((tall, wide), BF16),
            pltpu.VMEM((tall, wide), BF16),
            pltpu.VMEM((tall, clusters), F32),
            pltpu.VMEM((8, clusters), F32),
            pltpu.VMEM((ITERS, 7, SUB, clusters), F32),
            pltpu.VMEM((ITERS, 24, 8, clusters), F32),
            dma((9,)),
            dma((24,)),
            dma((24,)),
            dma((ITERS, 24)),
            dma((ITERS, 24)),
            dma((ITERS, 7)),
            dma((ITERS, 7)),
            dma((ITERS, 9)),
            dma((ITERS, 9)),
            dma((ITERS, 2, 16)),
            dma((ITERS, 2, 16)),
        ],
        compiler_params=pltpu.CompilerParams(
            collective_id=0, has_side_effects=True, vmem_limit_bytes=62 * 1024 * 1024
        ),
    )(features, logits)


def solution(mesh):
    return jax.shard_map(
        on_device,
        mesh=mesh,
        in_specs=(P("row", None), P(("row", "col"), None)),
        out_specs=(P(("row", "col"), None), P(("row", "col"), None)),
        check_vma=False,
    )
```

```python
import jax
import jax.numpy as jnp
from jax import lax
from jax.experimental import pallas as pl
from jax.experimental.pallas import tpu as pltpu
from jax.sharding import PartitionSpec as P

ITERS = 2
SUB = 256
MESH = pl.DeviceIdType.MESH
BF16 = jnp.bfloat16
F32 = jnp.float32


def rows(start, size=SUB):
    return pl.ds(start if isinstance(start, int) else pl.multiple_of(start, 128), size)


def softmax_rows(raised):
    return raised / jnp.sum(raised, axis=1, keepdims=True)


def kernel(
    feat, logits, memb_out, std_out,
    frow, fcol, mem0, mem1, rows0, rows1, p_hi, p_lo, total, wsum,
    inbox, vec,
    load_sem, f_send, f_recv, m_send, m_recv, a_send, a_recv, r_send, r_recv, v_send, v_recv,
):
    clusters = logits.shape[1]
    width = feat.shape[1]
    row, col = lax.axis_index("row"), lax.axis_index("col")
    z, xh = row // 2, row % 2
    y, xl, core = col // 4, (col // 2) % 2, col % 2

    def device(dz=0, dx1=0, dy=0, dx2=0, dk=0):
        new_xh = (xh + dx1) % 2
        new_xl = (xl + dx1 + dx2) % 2
        return (
            ((z + dz) % 4) * 2 + new_xh,
            ((y + dy) % 4) * 4 + new_xl * 2 + (core + dk) % 2,
        )

    z_up, z_down, z_far = device(dz=1), device(dz=3), device(dz=2)
    cross, partner = device(dx1=1), device(dk=1)
    y_up, y_down, y_far, across = device(dy=1), device(dy=3), device(dy=2), device(dx2=1)
    reduce_group = [(2, 1), (2, 0), (1, 1), (3, 1), (1, 0), (3, 0), (0, 1)]
    gather_group = [(dz, dx, dk) for dz in (2, 1, 3, 0) for dx in (1, 0) for dk in (1, 0)][:-1]

    barrier = pltpu.get_barrier_semaphore()
    nearest = (z_up, z_down, cross, partner, y_up, y_down, across)
    for where in nearest:
        pl.semaphore_signal(barrier, inc=1, device_id=where, device_id_type=MESH)

    order = [(2, 1), (1, 1), (3, 1), (1, 0), (3, 0), (2, 0), (0, 1), (0, 0)]
    loads = []
    for u, (dy, dx) in enumerate(order):
        block = ((y + dy) % 4) * 4 + ((xl + dx) % 2) * 2 + core
        loads.append(
            pltpu.make_async_copy(
                feat.at[rows(block * SUB)], frow.at[rows(u * SUB)], load_sem.at[u]
            )
        )
    loads.append(
        pltpu.make_async_copy(
            feat.at[rows((y * 4 + xl * 2) * SUB, 2 * SUB)], fcol.at[rows(0, 2 * SUB)], load_sem.at[8]
        )
    )
    for load in loads:
        load.start()

    def put_members(members, mem, tile_rows):
        hi = members.astype(BF16)
        lo = (members - hi.astype(F32)).astype(BF16)
        for ref, start in ((mem, core * SUB), (tile_rows, 7 * SUB)):
            ref[rows(start), 0:clusters] = hi
            ref[rows(start), clusters : 2 * clusters] = lo

    put_members(softmax_rows(jnp.exp(logits[...])), mem0, rows0)
    pl.semaphore_wait(barrier, len(nearest))

    class Stream:
        def __init__(self, buf, send, recv, halves, own_src=None):
            self.buf, self.send, self.recv, self.own_src = buf, send, recv, own_src
            self.halves = halves
            self.started = []

        def at(self, slot, half=None, other=False):
            start = slot * 2 * SUB + (1 - core if other else core) * SUB
            if half is None:
                return self.buf.at[rows(start)]
            return self.buf.at[rows(start + half * (SUB // 2), SUB // 2)]

        def own(self, half=None):
            if self.own_src is None:
                return self.at(0, half)
            start = self.own_src[1]
            if half is None:
                return self.own_src[0].at[rows(start)]
            return self.own_src[0].at[rows(start + half * (SUB // 2), SUB // 2)]

        def put(self, src, slot, where, half=None):
            n = len(self.started)
            self.started.append(src)
            sem = 16 + slot if where is partner else 2 * slot + (half or 0)
            pltpu.make_async_remote_copy(
                src_ref=src(), dst_ref=self.at(slot, half), send_sem=self.send.at[n],
                recv_sem=self.recv.at[sem], device_id=where, device_id_type=MESH,
            ).start()

        def wait(self, slot, half=None):
            dst = self.at(slot, half)
            pltpu.make_async_copy(dst, dst, self.recv.at[2 * slot + (half or 0)]).wait()

        def ready(self, *slots):
            for slot in slots:
                dst = self.at(slot, other=True)
                pltpu.make_async_copy(dst, dst, self.recv.at[16 + slot]).wait()

        def send_round(self):
            for first in range(2):
                self.put(lambda h=first: self.own(h), 3, z_up, first)
                self.put(lambda h=1 - first: self.own(h), 4, z_down, 1 - first)

        def ring(self):
            for slot, half, where in ((3, 0, z_up), (4, 1, z_down)):
                self.wait(slot, half)
                self.put(lambda slot=slot, half=half: self.at(slot, half), 2, where, half)

        def pass_on(self, slot, *where):
            for there, device_id in where:
                self.put(lambda: self.at(slot), there, device_id)
            self.put(lambda: self.at(slot), slot, partner)

        def relay(self, *slots):
            for slot in slots:
                if self.halves and slot == 2:
                    self.wait(2, 0)
                self.wait(slot, {2: 1, 3: 1, 4: 0}.get(slot) if self.halves else None)
                if slot == 1:
                    self.pass_on(1, (5, z_up), (6, z_down))
                elif slot == 2:
                    self.pass_on(2, (7, cross))
                else:
                    self.pass_on(slot)

        def finish(self):
            for n, src in enumerate(self.started):
                pltpu.make_async_copy(src(), src(), self.send.at[n]).wait()

    feats = Stream(fcol, f_send, f_recv, True, (feat, col * SUB))
    mems = [Stream(mem, m_send.at[i], m_recv.at[i], i == 1) for i, mem in enumerate((mem0, mem1))]

    def row_copy(it, dy, dx):
        there = order.index(((4 - dy) % 4, dx))
        buf = (rows0, rows1)[it]
        return pltpu.make_async_remote_copy(
            src_ref=buf.at[rows(7 * SUB)], dst_ref=buf.at[rows(there * SUB)],
            send_sem=a_send.at[it, there], recv_sem=a_recv.at[it, there],
            device_id=device(dy=dy, dx2=dx), device_id_type=MESH,
        )

    def send_rows(it, group):
        for dy, dx in group:
            row_copy(it, dy, dx).start()

    def wait_rows(it, group):
        for dy, dx in group:
            row_copy(it, (4 - dy) % 4, dx).wait_recv()

    row_near, row_mid, row_far = [(1, 0), (3, 0), (0, 1)], [(2, 0), (1, 1), (3, 1)], [(2, 1)]

    feats.send_round()
    feats.put(feats.own, 1, cross)
    mems[0].put(mems[0].own, 0, partner)
    mems[0].put(mems[0].own, 1, cross)
    send_rows(0, row_near)

    for load in loads:
        load.wait()

    def scale(i, carry):
        frow[rows(i * SUB), :] = frow[rows(i * SUB), :] * (1.0 / width)
        return carry

    lax.fori_loop(0, 8, scale, 0)

    def inner(first, last):
        def block(b, carry):
            at = rows(b * SUB)
            x = lax.dot_general(
                frow[...], fcol[at, :], (((1,), (1,)), ((), ())), preferred_element_type=F32
            )
            p = x * (3.0 + x * (3.0 + x))
            hi = p.astype(BF16)
            p_hi[:, at] = hi
            p_lo[:, at] = (p - hi.astype(F32)).astype(BF16)
            return carry

        lax.fori_loop(2 * first, 2 * last, block, 0)

    def product(at, cols, mem):
        both = jnp.dot(p_hi[at, cols], mem[cols, :], preferred_element_type=F32)
        low = jnp.dot(p_lo[at, cols], mem[cols, 0:clusters], preferred_element_type=F32)
        return both[:, :clusters] + both[:, clusters:] + low

    def column_pass(mem, first, last, actions=()):
        def chunk(i, carry):
            at = rows(i * 512, 512)
            part = product(at, slice(first * 2 * SUB, last * 2 * SUB), mem)
            total[at, :] = part if first == 0 else total[at, :] + part
            for step, action in actions:
                pl.when(i == step)(action)
            return carry

        lax.fori_loop(0, 4, chunk, 0)

    pending = []

    def exchange(values, buf, send, recv, group):
        buf[0] = values
        copies = [
            pltpu.make_async_remote_copy(
                src_ref=buf.at[0], dst_ref=buf.at[slot], send_sem=send.at[slot],
                recv_sem=recv.at[slot], device_id=where, device_id_type=MESH,
            )
            for where, slot in group
        ]
        for copy in copies:
            copy.start()
        pending.extend(copies)

        def finish():
            out = buf[0]
            for _, slot in group:
                pltpu.make_async_copy(buf.at[slot], buf.at[slot], recv.at[slot]).wait()
                out = out + buf[slot]
            return out

        return finish

    near_ids = [(device(dy=dy, dx2=dx), ((4 - dy) % 4) * 2 + dx) for dy, dx in reduce_group]
    far_ids = [
        (device(dz=dz, dx1=dx, dk=dk), ((4 - dz) % 4) * 4 + dx * 2 + dk) for dz, dx, dk in gather_group
    ]

    for it in range(ITERS):
        mem, stream, tile_rows = (mem0, mem1)[it], mems[it], (rows0, rows1)[it]
        row_all = row_near + row_mid + row_far
        if it == 0:
            inner(0, 1)
            feats.ring()
            stream.put(stream.own, 3, z_up)
            stream.put(stream.own, 4, z_down)
            stream.put(stream.own, 2, z_far)
            stream.ready(0)
            column_pass(mem, 0, 1)
            feats.relay(1, 3, 4)
            wait_rows(0, row_near)
            send_rows(0, row_mid)
            feats.ready(1)
            inner(1, 2)
            feats.relay(2)
            stream.relay(1)
            feats.ready(3, 4)
            inner(3, 5)
            wait_rows(0, row_mid)
            send_rows(0, row_far)
            stream.relay(2)
            feats.ready(2)
            inner(2, 3)
            stream.relay(3, 4)
            stream.ready(1, 2)
            column_pass(mem, 1, 3, [(3, lambda: feats.relay(7))])
            stream.ready(3, 4)
            column_pass(mem, 3, 5, [(1, lambda: feats.relay(5, 6)), (3, lambda: stream.relay(7))])
            feats.ready(7)
            inner(7, 8)
            stream.relay(5, 6)
            feats.ready(5, 6)
            inner(5, 7)
        else:
            stream.put(stream.own, 0, partner)
            stream.send_round()
            stream.put(stream.own, 1, cross)
            send_rows(it, row_all)
            stream.ready(0)
            column_pass(mem, 0, 1)
            stream.ring()
            stream.relay(1, 3, 4, 2)
            stream.ready(1)
            column_pass(mem, 1, 2)
            stream.ready(2, 3, 4)
            column_pass(mem, 2, 5, [(1, lambda: stream.relay(5, 6)), (2, lambda: stream.relay(7))])
        stream.ready(5, 6, 7)

        def score_copy(n):
            u, slot, start, size, where = routes[n]
            return pltpu.make_async_remote_copy(
                src_ref=total.at[rows(u * SUB + start, size)], dst_ref=inbox.at[it, slot, pl.ds(start, size)],
                send_sem=r_send.at[it, n], recv_sem=r_recv.at[it, n],
                device_id=where, device_id_type=MESH,
            )

        half = SUB // 2
        routes = [
            (0, 0, 0, SUB, across), (1, 1, 0, SUB, y_up), (2, 2, 0, SUB, y_down),
            (3, 3, 0, half, y_up), (4, 4, 0, half, y_down), (5, 5, 0, SUB, y_far), (6, 6, 0, SUB, across),
            (3, 3, half, half, y_up), (4, 4, half, half, y_down),
        ]

        def of(ref, at):
            return ref[at, 0:clusters].astype(F32) + ref[at, clusters : 2 * clusters].astype(F32)

        def fold(values):
            return jnp.sum(values.reshape(SUB // 8, 8, clusters), axis=0)

        wait_rows(it, row_far if it == 0 else row_all)
        wsum[...] = jnp.zeros_like(wsum)

        def step(u, carry):
            at = rows(u * SUB)
            part = total[at, :] + product(at, slice(5 * 2 * SUB, 8 * 2 * SUB), mem)
            total[at, :] = part
            wsum[...] += fold(of(tile_rows, at) * part)
            for v in range(5):
                pl.when(u == v)(lambda v=v: score_copy(v).start())
            return carry

        lax.fori_loop(0, 8, step, 0)
        sizes = fold(of(tile_rows, rows(7 * SUB)))
        first = lax.broadcasted_iota(jnp.int32, (8, clusters), 0) == 0
        sums_done = exchange(
            jnp.where(
                first, jnp.sum(wsum[...], axis=0, keepdims=True), jnp.sum(sizes, axis=0, keepdims=True)
            ),
            vec.at[it, pl.ds(0, 16)], v_send.at[it, 0], v_recv.at[it, 0], far_ids,
        )
        score_copy(0).wait_recv()
        total[rows(5 * SUB), :] = total[rows(5 * SUB), :] + inbox[it, 0]
        score_copy(5).start()
        score_copy(1).wait_recv()
        score_copy(2).wait_recv()
        total[rows(6 * SUB), :] = total[rows(6 * SUB), :] + inbox[it, 1] + inbox[it, 2]
        score_copy(6).start()
        score_copy(7).start()
        score_copy(8).start()
        sums_done = exchange(
            sums_done(), vec.at[it, pl.ds(16, 8)], v_send.at[it, 1], v_recv.at[it, 1], near_ids,
        )
        sums = sums_done()
        weighted, size = sums[0:1], sums[1:2]
        for n in range(3, 9):
            score_copy(n).wait_recv()
        scores = total[rows(7 * SUB), :]
        for slot in range(3, 7):
            scores = scores + inbox[it, slot]
        distance = weighted / (size * size) - 2.0 * scores / size
        centered = distance - jnp.mean(distance, axis=1, keepdims=True)
        spread = jnp.mean(centered * centered, axis=1, keepdims=True)
        standardized = centered / jnp.sqrt(spread + 1e-06)
        members = softmax_rows(jnp.exp(-2.0 * standardized))
        for n in range(9):
            score_copy(n).wait_send()
        for copy in pending:
            copy.wait_send()
        pending.clear()
        if it + 1 < ITERS:
            put_members(members, mem1, rows1)
        else:
            memb_out[...] = members
            std_out[...] = standardized
    for it in range(ITERS):
        mems[it].finish()
        for dy, dx in row_near + row_mid + row_far:
            row_copy(it, dy, dx).wait_send()
    feats.finish()


def on_device(features, logits):
    frames, clusters = logits.shape
    width = features.shape[1]
    tall, wide = 8 * SUB, 16 * SUB
    vmem = pl.BlockSpec(memory_space=pltpu.VMEM)
    out = jax.ShapeDtypeStruct((frames, clusters), F32)
    dma = pltpu.SemaphoreType.DMA
    return pl.pallas_call(
        kernel,
        out_shape=(out, out),
        in_specs=[pl.BlockSpec(memory_space=pl.ANY), vmem],
        out_specs=(vmem, vmem),
        scratch_shapes=[
            pltpu.VMEM((tall, width), BF16),
            pltpu.VMEM((wide, width), BF16),
            pltpu.VMEM((wide, 2 * clusters), BF16),
            pltpu.VMEM((wide, 2 * clusters), BF16),
            pltpu.VMEM((tall, 2 * clusters), BF16),
            pltpu.VMEM((tall, 2 * clusters), BF16),
            pltpu.VMEM((tall, wide), BF16),
            pltpu.VMEM((tall, wide), BF16),
            pltpu.VMEM((tall, clusters), F32),
            pltpu.VMEM((8, clusters), F32),
            pltpu.VMEM((ITERS, 7, SUB, clusters), F32),
            pltpu.VMEM((ITERS, 24, 8, clusters), F32),
            dma((9,)),
            dma((24,)),
            dma((24,)),
            dma((ITERS, 24)),
            dma((ITERS, 24)),
            dma((ITERS, 7)),
            dma((ITERS, 7)),
            dma((ITERS, 9)),
            dma((ITERS, 9)),
            dma((ITERS, 2, 16)),
            dma((ITERS, 2, 16)),
        ],
        compiler_params=pltpu.CompilerParams(
            collective_id=0, has_side_effects=True, vmem_limit_bytes=62 * 1024 * 1024
        ),
    )(features, logits)


def solution(mesh):
    return jax.shard_map(
        on_device,
        mesh=mesh,
        in_specs=(P("row", None), P(("row", "col"), None)),
        out_specs=(P(("row", "col"), None), P(("row", "col"), None)),
        check_vma=False,
    )
```

```python
import jax
import jax.numpy as jnp
from jax import lax
from jax.experimental import pallas as pl
from jax.experimental.pallas import tpu as pltpu
from jax.sharding import PartitionSpec as P

ITERS = 2
SUB = 256
MESH = pl.DeviceIdType.MESH
BF16 = jnp.bfloat16
F32 = jnp.float32


def rows(start, size=SUB):
    return pl.ds(start if isinstance(start, int) else pl.multiple_of(start, 128), size)


def softmax_rows(raised):
    return raised * (1.0 / jnp.sum(raised, axis=1, keepdims=True))


def kernel(
    feat, logits, memb_out, std_out,
    frow, fcol, mem0, mem1, rows0, rows1, p_hi, p_lo, total, wsum,
    inbox, vec,
    load_sem, f_send, f_recv, m_send, m_recv, a_send, a_recv, r_send, r_recv, v_send, v_recv,
):
    clusters = logits.shape[1]
    width = feat.shape[1]
    row, col = lax.axis_index("row"), lax.axis_index("col")
    z, xh = row // 2, row % 2
    y, xl, core = col // 4, (col // 2) % 2, col % 2

    def device(dz=0, dx1=0, dy=0, dx2=0, dk=0):
        new_xh = (xh + dx1) % 2
        new_xl = (xl + dx1 + dx2) % 2
        return (
            ((z + dz) % 4) * 2 + new_xh,
            ((y + dy) % 4) * 4 + new_xl * 2 + (core + dk) % 2,
        )

    z_up, z_down, z_far = device(dz=1), device(dz=3), device(dz=2)
    cross, partner = device(dx1=1), device(dk=1)
    y_up, y_down, y_far, across = device(dy=1), device(dy=3), device(dy=2), device(dx2=1)
    reduce_group = [(2, 1), (2, 0), (1, 1), (3, 1), (1, 0), (3, 0), (0, 1)]
    gather_group = [(dz, dx, dk) for dz in (2, 1, 3, 0) for dx in (1, 0) for dk in (1, 0)][:-1]

    barrier = pltpu.get_barrier_semaphore()
    nearest = (z_up, z_down, cross, partner, y_up, y_down, across)
    for where in nearest:
        pl.semaphore_signal(barrier, inc=1, device_id=where, device_id_type=MESH)

    order = [(2, 1), (1, 1), (3, 1), (1, 0), (3, 0), (2, 0), (0, 1), (0, 0)]
    loads = []
    for u, (dy, dx) in enumerate(order):
        block = ((y + dy) % 4) * 4 + ((xl + dx) % 2) * 2 + core
        loads.append(
            pltpu.make_async_copy(
                feat.at[rows(block * SUB)], frow.at[rows(u * SUB)], load_sem.at[u]
            )
        )
    loads.append(
        pltpu.make_async_copy(
            feat.at[rows((y * 4 + xl * 2) * SUB, 2 * SUB)], fcol.at[rows(0, 2 * SUB)], load_sem.at[8]
        )
    )
    for load in loads:
        load.start()

    def put_members(members, mem, tile_rows):
        hi = members.astype(BF16)
        lo = (members - hi.astype(F32)).astype(BF16)
        for ref, start in ((mem, core * SUB), (tile_rows, 7 * SUB)):
            ref[rows(start), 0:clusters] = hi
            ref[rows(start), clusters : 2 * clusters] = lo

    put_members(softmax_rows(jnp.exp(logits[...])), mem0, rows0)
    pl.semaphore_wait(barrier, len(nearest))

    class Stream:
        def __init__(self, buf, send, recv, halves, own_src=None):
            self.buf, self.send, self.recv, self.own_src = buf, send, recv, own_src
            self.halves = halves
            self.started = []

        def at(self, slot, half=None, other=False):
            start = slot * 2 * SUB + (1 - core if other else core) * SUB
            if half is None:
                return self.buf.at[rows(start)]
            return self.buf.at[rows(start + half * (SUB // 2), SUB // 2)]

        def own(self, half=None):
            if self.own_src is None:
                return self.at(0, half)
            start = self.own_src[1]
            if half is None:
                return self.own_src[0].at[rows(start)]
            return self.own_src[0].at[rows(start + half * (SUB // 2), SUB // 2)]

        def put(self, src, slot, where, half=None):
            n = len(self.started)
            self.started.append(src)
            sem = 16 + slot if where is partner else 2 * slot + (half or 0)
            pltpu.make_async_remote_copy(
                src_ref=src(), dst_ref=self.at(slot, half), send_sem=self.send.at[n],
                recv_sem=self.recv.at[sem], device_id=where, device_id_type=MESH,
            ).start()

        def wait(self, slot, half=None):
            dst = self.at(slot, half)
            pltpu.make_async_copy(dst, dst, self.recv.at[2 * slot + (half or 0)]).wait()

        def ready(self, *slots):
            for slot in slots:
                dst = self.at(slot, other=True)
                pltpu.make_async_copy(dst, dst, self.recv.at[16 + slot]).wait()

        def send_round(self):
            for first in range(2):
                self.put(lambda h=first: self.own(h), 3, z_up, first)
                self.put(lambda h=1 - first: self.own(h), 4, z_down, 1 - first)

        def ring(self):
            for slot, half, where in ((3, 0, z_up), (4, 1, z_down)):
                self.wait(slot, half)
                self.put(lambda slot=slot, half=half: self.at(slot, half), 2, where, half)

        def pass_on(self, slot, *where):
            for there, device_id in where:
                self.put(lambda: self.at(slot), there, device_id)
            self.put(lambda: self.at(slot), slot, partner)

        def relay(self, *slots):
            for slot in slots:
                if self.halves and slot == 2:
                    self.wait(2, 0)
                self.wait(slot, {2: 1, 3: 1, 4: 0}.get(slot) if self.halves else None)
                if slot == 1:
                    self.pass_on(1, (5, z_up), (6, z_down))
                elif slot == 2:
                    self.pass_on(2, (7, cross))
                else:
                    self.pass_on(slot)

        def finish(self):
            for n, src in enumerate(self.started):
                pltpu.make_async_copy(src(), src(), self.send.at[n]).wait()

    feats = Stream(fcol, f_send, f_recv, True, (feat, col * SUB))
    mems = [Stream(mem, m_send.at[i], m_recv.at[i], i == 1) for i, mem in enumerate((mem0, mem1))]

    def row_copy(it, dy, dx):
        there = order.index(((4 - dy) % 4, dx))
        buf = (rows0, rows1)[it]
        return pltpu.make_async_remote_copy(
            src_ref=buf.at[rows(7 * SUB)], dst_ref=buf.at[rows(there * SUB)],
            send_sem=a_send.at[it, there], recv_sem=a_recv.at[it, there],
            device_id=device(dy=dy, dx2=dx), device_id_type=MESH,
        )

    def send_rows(it, group):
        for dy, dx in group:
            row_copy(it, dy, dx).start()

    def wait_rows(it, group):
        for dy, dx in group:
            row_copy(it, (4 - dy) % 4, dx).wait_recv()

    row_near, row_mid, row_far = [(1, 0), (3, 0), (0, 1)], [(2, 0), (1, 1), (3, 1)], [(2, 1)]

    feats.send_round()
    feats.put(feats.own, 1, cross)
    mems[0].put(mems[0].own, 0, partner)
    mems[0].put(mems[0].own, 1, cross)
    send_rows(0, row_near)

    for load in loads:
        load.wait()

    def scale(i, carry):
        frow[rows(i * SUB), :] = frow[rows(i * SUB), :] * (1.0 / width)
        return carry

    lax.fori_loop(0, 8, scale, 0)

    def inner(first, last):
        def block(b, carry):
            at = rows(b * SUB)
            x = lax.dot_general(
                frow[...], fcol[at, :], (((1,), (1,)), ((), ())), preferred_element_type=F32
            )
            p = x * (3.0 + x * (3.0 + x))
            hi = p.astype(BF16)
            p_hi[:, at] = hi
            p_lo[:, at] = (p - hi.astype(F32)).astype(BF16)
            return carry

        lax.fori_loop(2 * first, 2 * last, block, 0)

    def product(at, cols, mem):
        both = jnp.dot(p_hi[at, cols], mem[cols, :], preferred_element_type=F32)
        low = jnp.dot(p_lo[at, cols], mem[cols, 0:clusters], preferred_element_type=F32)
        return both[:, :clusters] + both[:, clusters:] + low

    def column_pass(mem, first, last, actions=()):
        def chunk(i, carry):
            at = rows(i * 512, 512)
            part = product(at, slice(first * 2 * SUB, last * 2 * SUB), mem)
            total[at, :] = part if first == 0 else total[at, :] + part
            for step, action in actions:
                pl.when(i == step)(action)
            return carry

        lax.fori_loop(0, 4, chunk, 0)

    pending = []

    def exchange(values, buf, send, recv, group):
        buf[0] = values
        copies = [
            pltpu.make_async_remote_copy(
                src_ref=buf.at[0], dst_ref=buf.at[slot], send_sem=send.at[slot],
                recv_sem=recv.at[slot], device_id=where, device_id_type=MESH,
            )
            for where, slot in group
        ]
        for copy in copies:
            copy.start()
        pending.extend(copies)

        def finish():
            out = buf[0]
            for _, slot in group:
                pltpu.make_async_copy(buf.at[slot], buf.at[slot], recv.at[slot]).wait()
                out = out + buf[slot]
            return out

        return finish

    near_ids = [(device(dy=dy, dx2=dx), ((4 - dy) % 4) * 2 + dx) for dy, dx in reduce_group]
    far_ids = [
        (device(dz=dz, dx1=dx, dk=dk), ((4 - dz) % 4) * 4 + dx * 2 + dk) for dz, dx, dk in gather_group
    ]

    for it in range(ITERS):
        mem, stream, tile_rows = (mem0, mem1)[it], mems[it], (rows0, rows1)[it]
        row_all = row_near + row_mid + row_far
        if it == 0:
            inner(0, 1)
            feats.ring()
            stream.put(stream.own, 3, z_up)
            stream.put(stream.own, 4, z_down)
            stream.put(stream.own, 2, z_far)
            stream.ready(0)
            column_pass(mem, 0, 1)
            feats.relay(1, 3, 4)
            wait_rows(0, row_near)
            send_rows(0, row_mid)
            feats.ready(1)
            inner(1, 2)
            feats.relay(2)
            stream.relay(1)
            feats.ready(3, 4)
            inner(3, 5)
            wait_rows(0, row_mid)
            send_rows(0, row_far)
            stream.relay(2)
            feats.ready(2)
            inner(2, 3)
            stream.relay(3, 4)
            stream.ready(1, 2)
            column_pass(mem, 1, 3, [(3, lambda: feats.relay(7))])
            stream.ready(3, 4)
            column_pass(mem, 3, 5, [(1, lambda: feats.relay(5, 6)), (3, lambda: stream.relay(7))])
            feats.ready(7)
            inner(7, 8)
            stream.relay(5, 6)
            feats.ready(5, 6)
            inner(5, 7)
        else:
            stream.put(stream.own, 0, partner)
            stream.send_round()
            stream.put(stream.own, 1, cross)
            send_rows(it, row_all)
            stream.ready(0)
            column_pass(mem, 0, 1)
            stream.ring()
            stream.relay(1, 3, 4, 2)
            stream.ready(1)
            column_pass(mem, 1, 2)
            stream.ready(2, 3, 4)
            column_pass(mem, 2, 5, [(1, lambda: stream.relay(5, 6)), (2, lambda: stream.relay(7))])
        stream.ready(5, 6, 7)

        def score_copy(n):
            u, slot, start, size, where = routes[n]
            return pltpu.make_async_remote_copy(
                src_ref=total.at[rows(u * SUB + start, size)], dst_ref=inbox.at[it, slot, pl.ds(start, size)],
                send_sem=r_send.at[it, n], recv_sem=r_recv.at[it, n],
                device_id=where, device_id_type=MESH,
            )

        half = SUB // 2
        routes = [
            (0, 0, 0, SUB, across), (1, 1, 0, SUB, y_up), (2, 2, 0, SUB, y_down),
            (3, 3, 0, half, y_up), (4, 4, 0, half, y_down), (5, 5, 0, SUB, y_far), (6, 6, 0, SUB, across),
            (3, 3, half, half, y_up), (4, 4, half, half, y_down),
        ]

        def of(ref, at):
            return ref[at, 0:clusters].astype(F32) + ref[at, clusters : 2 * clusters].astype(F32)

        def fold(values):
            return jnp.sum(values.reshape(SUB // 8, 8, clusters), axis=0)

        wait_rows(it, row_far if it == 0 else row_all)
        wsum[...] = jnp.zeros_like(wsum)

        def step(u, carry):
            at = rows(u * SUB)
            part = total[at, :] + product(at, slice(5 * 2 * SUB, 8 * 2 * SUB), mem)
            total[at, :] = part
            wsum[...] += fold(of(tile_rows, at) * part)
            for v in range(5):
                pl.when(u == v)(lambda v=v: score_copy(v).start())
            return carry

        lax.fori_loop(0, 8, step, 0)
        sizes = fold(of(tile_rows, rows(7 * SUB)))
        first = lax.broadcasted_iota(jnp.int32, (8, clusters), 0) == 0
        sums_done = exchange(
            jnp.where(
                first, jnp.sum(wsum[...], axis=0, keepdims=True), jnp.sum(sizes, axis=0, keepdims=True)
            ),
            vec.at[it, pl.ds(0, 16)], v_send.at[it, 0], v_recv.at[it, 0], far_ids,
        )
        score_copy(0).wait_recv()
        total[rows(5 * SUB), :] = total[rows(5 * SUB), :] + inbox[it, 0]
        score_copy(5).start()
        score_copy(1).wait_recv()
        score_copy(2).wait_recv()
        total[rows(6 * SUB), :] = total[rows(6 * SUB), :] + inbox[it, 1] + inbox[it, 2]
        score_copy(6).start()
        score_copy(7).start()
        score_copy(8).start()
        sums_done = exchange(
            sums_done(), vec.at[it, pl.ds(16, 8)], v_send.at[it, 1], v_recv.at[it, 1], near_ids,
        )
        sums = sums_done()
        weighted, size = sums[0:1], sums[1:2]
        for n in range(3, 9):
            score_copy(n).wait_recv()
        scores = total[rows(7 * SUB), :]
        for slot in range(3, 7):
            scores = scores + inbox[it, slot]
        distance = weighted / (size * size) - scores * (2.0 / size)
        centered = distance - jnp.mean(distance, axis=1, keepdims=True)
        spread = jnp.mean(centered * centered, axis=1, keepdims=True)
        standardized = centered * (1.0 / jnp.sqrt(spread + 1e-06))
        members = softmax_rows(jnp.exp(-2.0 * standardized))
        for n in range(9):
            score_copy(n).wait_send()
        for copy in pending:
            copy.wait_send()
        pending.clear()
        if it + 1 < ITERS:
            put_members(members, mem1, rows1)
        else:
            memb_out[...] = members
            std_out[...] = standardized
    for it in range(ITERS):
        mems[it].finish()
        for dy, dx in row_near + row_mid + row_far:
            row_copy(it, dy, dx).wait_send()
    feats.finish()


def on_device(features, logits):
    frames, clusters = logits.shape
    width = features.shape[1]
    tall, wide = 8 * SUB, 16 * SUB
    vmem = pl.BlockSpec(memory_space=pltpu.VMEM)
    out = jax.ShapeDtypeStruct((frames, clusters), F32)
    dma = pltpu.SemaphoreType.DMA
    return pl.pallas_call(
        kernel,
        out_shape=(out, out),
        in_specs=[pl.BlockSpec(memory_space=pl.ANY), vmem],
        out_specs=(vmem, vmem),
        scratch_shapes=[
            pltpu.VMEM((tall, width), BF16),
            pltpu.VMEM((wide, width), BF16),
            pltpu.VMEM((wide, 2 * clusters), BF16),
            pltpu.VMEM((wide, 2 * clusters), BF16),
            pltpu.VMEM((tall, 2 * clusters), BF16),
            pltpu.VMEM((tall, 2 * clusters), BF16),
            pltpu.VMEM((tall, wide), BF16),
            pltpu.VMEM((tall, wide), BF16),
            pltpu.VMEM((tall, clusters), F32),
            pltpu.VMEM((8, clusters), F32),
            pltpu.VMEM((ITERS, 7, SUB, clusters), F32),
            pltpu.VMEM((ITERS, 24, 8, clusters), F32),
            dma((9,)),
            dma((24,)),
            dma((24,)),
            dma((ITERS, 24)),
            dma((ITERS, 24)),
            dma((ITERS, 7)),
            dma((ITERS, 7)),
            dma((ITERS, 9)),
            dma((ITERS, 9)),
            dma((ITERS, 2, 16)),
            dma((ITERS, 2, 16)),
        ],
        compiler_params=pltpu.CompilerParams(
            collective_id=0, has_side_effects=True, vmem_limit_bytes=62 * 1024 * 1024
        ),
    )(features, logits)


def solution(mesh):
    return jax.shard_map(
        on_device,
        mesh=mesh,
        in_specs=(P("row", None), P(("row", "col"), None)),
        out_specs=(P(("row", "col"), None), P(("row", "col"), None)),
        check_vma=False,
    )
```
